32 devices in a mesh: grp: 4 (over x, core), leaf: 8 (over z, y).
Axes of the slice: x: 2, y: 2, z: 4, core: 2. Of those that a mesh axis runs over, the one named last changes fastest.
Arguments:
- matrix: bfloat16 [8192, 8192], P('grp', 'leaf'), may hold values from -0.09375 to 0.09375
- probes: bfloat16 [8192, 512], P('leaf'), may hold values from -6 to 6
- leaf_skeleton: int32 [32, 128], P(('grp', 'leaf')), may hold values from 0 to 255, as said below
- node_skeleton: int32 [31, 128], replicated, may hold values from 0 to 255, as said below
Outputs:
- leaf_basis: float32 [8192, 128], P(('grp', 'leaf'))
- transfer: float32 [32, 256, 128], P(('grp', 'leaf'))
The draws below stay inside these ranges and needn't reach their ends.
Inputs may be any that keep to these rules, and one draw needn't show every extreme that they name: `leaf_skeleton`: each row holds 128 distinct increasing row numbers within one leaf. `node_skeleton`: each row holds 128 distinct increasing numbers into the node's stacked rows, the first child's 128 rows first.
All inputs are finite; a program needn't handle non-finite values.
Results may differ from the reference program's by a relative error of at most 0.0003.
Values sent between devices are 32-bit elements; how exact they have to be, the bound alone decides.
No kernel may reach another device: no remote copies, remote signals or barrier semaphores. Data moves between devices by JAX's collectives and lax.ppermute only.
A program may use at most 128 MiB of HBM per device.

```python
import jax
import jax.numpy as jnp
from jax import lax

LR = 256
RANK = 128
S = 512
LEAVES = 32
N = 8192
N_LEAF = 8


def draw_leaf_skeleton(key, part):
    keys = jax.random.split(jax.random.fold_in(key, 11), LEAVES)
    picks = jax.vmap(lambda k: jnp.sort(jax.random.permutation(k, LR)[:RANK]))(keys)
    return picks.astype(jnp.int32)


def draw_node_skeleton(key, part):
    keys = jax.random.split(jax.random.fold_in(key, 23), LEAVES - 1)
    picks = jax.vmap(lambda k: jnp.sort(jax.random.permutation(k, 2 * RANK)[:RANK]))(keys)
    return picks.astype(jnp.int32)


def strengthened(values, stream_key, source, target, blocks, factor):
    def block_of(dim):
        return (jnp.arange(values.shape[dim]) // (values.shape[dim] // blocks)).reshape((-1,) + (1,) * (values.ndim - 1 - dim))

    one_side = jax.random.permutation(stream_key, blocks)[block_of(target)]
    second = (block_of(target) + blocks // 2) % blocks
    return jnp.where((block_of(source) == one_side) | (block_of(source) == second), factor * values, values)


def steps_of(key, extent, cuts, low, top_value):
    level, own = 1.0, jax.random.fold_in(key, 6)
    for dim, shards_of in cuts:
        steps = jnp.exp(jax.random.uniform(jax.random.fold_in(own, dim), (shards_of,), jnp.float32, low / len(cuts), top_value / len(cuts)))
        level = level * jnp.repeat(steps, extent[dim] // shards_of).reshape([-1 if axis == dim else 1 for axis in range(len(extent))])
    return level


def gaussian(own_key, extent, deviation, limit, cuts=(), held_as=jnp.bfloat16):
    values = deviation * jax.random.normal(own_key, extent, jnp.float32)
    if cuts:
        values = values * steps_of(own_key, extent, cuts, -0.22, 0.18)
    return jnp.clip(values, -limit, limit).astype(held_as)


def bell_draw_with(own_key, dims, width, limit, cuts, heavy, kind=jnp.bfloat16):
    result = width * jax.random.normal(own_key, dims, jnp.float32)
    if cuts:
        result = result * steps_of(own_key, dims, cuts, -0.22, 0.18)
    return jnp.clip(strengthened(result, jax.random.fold_in(own_key, 3), *heavy), -limit, limit).astype(kind)


def setup_inputs(seed: int = 0) -> dict:
    key_list = jax.random.split(jax.random.key(seed), 5)
    return {
        "matrix": bell_draw_with(key_list[0], (N, N), N ** -0.5, 0.09375, ((0, 4), (1, 8)), (1, 0, 8, 2.0)),
        "probes": gaussian(key_list[1], (N, S), 1.0, 6.0, ((0, 8),)),
        "leaf_skeleton": draw_leaf_skeleton(jax.random.fold_in(key_list[4], 71), 0),
        "node_skeleton": draw_node_skeleton(jax.random.fold_in(key_list[4], 71), 0),
    }


def node_bases(stacked, picked):
    rows = jnp.take_along_axis(stacked, picked[:, :, None], axis=1)
    gram = jnp.einsum('nks,nls->nkl', rows, rows, precision=lax.Precision.HIGHEST)
    cross = jnp.einsum('nks,nis->nki', rows, stacked, precision=lax.Precision.HIGHEST)
    factor = jnp.linalg.cholesky(gram)
    first = lax.linalg.triangular_solve(factor, cross, left_side=True, lower=True)
    solved = lax.linalg.triangular_solve(factor, first, left_side=True, lower=True, transpose_a=True)
    return (jnp.swapaxes(solved, 1, 2), rows)

def reference(matrix, probes, leaf_skeleton, node_skeleton):
    cols = N // N_LEAF
    row_leaf = jnp.arange(N, dtype=jnp.int32) // LR

    def add_block(block_index, total):
        start = (block_index * cols).astype(jnp.int32)
        block = lax.dynamic_slice_in_dim(matrix, start, cols, 1)
        col_leaf = (start + jnp.arange(cols, dtype=jnp.int32)) // LR
        keep = row_leaf[:, None] != col_leaf[None, :]
        block = jnp.where(keep, block, jnp.zeros((), matrix.dtype))
        probe_rows = lax.dynamic_slice_in_dim(probes, start, cols, 0)
        part = jnp.dot(block.astype(jnp.float32), probe_rows.astype(jnp.float32), preferred_element_type=jnp.float32)
        return total + part
    samples = lax.fori_loop(jnp.int32(0), jnp.int32(N_LEAF), add_block, jnp.zeros((N, S), jnp.float32))
    leaves = samples.reshape(LEAVES, LR, S)
    basis, carried = node_bases(leaves, leaf_skeleton)
    leaf_basis = basis.reshape(N, RANK)
    levels = int(LEAVES).bit_length() - 1
    uppers = []
    offset = 0
    count = LEAVES
    for level in range(levels):
        count = count // 2
        stacked = carried.reshape(count, 2 * RANK, S)
        picked = node_skeleton[offset:offset + count]
        upper, carried = node_bases(stacked, picked)
        uppers.append(upper)
        offset = offset + count
    table = []
    for device in range(LEAVES):
        if device == 0:
            level = levels
        else:
            level = (device & -device).bit_length()
        table.append(uppers[level - 1][device >> level])
    return (leaf_basis, jnp.stack(table))
```

```python
import jax
import jax.numpy as jnp
from jax import lax
from jax.experimental import pallas as pl
from jax.experimental.pallas import tpu as pltpu
from jax.sharding import PartitionSpec as P

HIGHEST = lax.Precision.HIGHEST


def bits_of(count):
    return count.bit_length() - 1


def spd_inverse(a):
    n = a.shape[0]
    rows = lax.broadcasted_iota(jnp.int32, (n, n), 0)
    cols = lax.broadcasted_iota(jnp.int32, (n, n), 1)
    lane = cols[:1]
    for k in range(0, n, 2):
        r0 = a[k : k + 1, :]
        r1 = a[k + 1 : k + 2, :]
        c0 = jnp.broadcast_to(a[:, k : k + 1], (n, n))
        c1 = jnp.broadcast_to(a[:, k + 1 : k + 2], (n, n))
        p = jnp.broadcast_to(a[k : k + 1, k : k + 1], (1, n))
        q = jnp.broadcast_to(a[k : k + 1, k + 1 : k + 2], (1, n))
        s = jnp.broadcast_to(a[k + 1 : k + 2, k + 1 : k + 2], (1, n))
        inv = 1.0 / (p * s - q * q)
        ip, iq, js = s * inv, -q * inv, p * inv
        w0 = ip * r0 + iq * r1
        w1 = iq * r0 + js * r1
        upd = a - c0 * jnp.broadcast_to(w0, (n, n)) - c1 * jnp.broadcast_to(w1, (n, n))
        k0 = -(c0 * ip + c1 * iq)
        k1 = -(c0 * iq + c1 * js)
        upd = jnp.where(cols == k, k0, jnp.where(cols == k + 1, k1, upd))
        x0 = jnp.where(lane == k, ip, jnp.where(lane == k + 1, iq, w0))
        x1 = jnp.where(lane == k, iq, jnp.where(lane == k + 1, js, w1))
        upd = jnp.where(rows == k + 1, jnp.broadcast_to(x1, (n, n)), upd)
        a = jnp.where(rows == k, jnp.broadcast_to(x0, (n, n)), upd)
    return a


def basis_kernel(own_ref, received_ref, picked_ref, basis_ref):
    cross = own_ref[...] + received_ref[...]
    index = lax.broadcasted_iota(jnp.int32, cross.shape, 0)
    choice = (index == picked_ref[...]).astype(jnp.float32)
    gram = lax.dot_general(
        choice,
        cross,
        (((0,), (0,)), ((), ())),
        precision=HIGHEST,
        preferred_element_type=jnp.float32,
    )
    basis_ref[...] = jnp.dot(
        cross, spd_inverse(gram), precision=HIGHEST, preferred_element_type=jnp.float32
    )


def basis_of(own, received, picked):
    return pl.pallas_call(
        basis_kernel,
        out_shape=jax.ShapeDtypeStruct(own.shape, jnp.float32),
        name="basis",
    )(own, received, picked[None])


def product_kernel(n_leaf, n_grp, place_ref, matrix_ref, probes_ref, send_ref, keep_ref):
    step = pl.program_id(0)
    leaf = place_ref[1] * n_leaf + 2 * place_ref[0] + step
    hit = leaf - place_ref[2] * n_grp
    side = place_ref[2] & 1
    rows = matrix_ref.shape[0]
    half = send_ref.shape[1]
    pieces = []
    for c in range(n_grp):
        piece = matrix_ref[:, c * rows : (c + 1) * rows]
        pieces.append(jnp.where(hit == c, jnp.zeros_like(piece), piece))
    block = jnp.concatenate(pieces, axis=1)
    away = pl.multiple_of((1 - side) * half, half)
    home = pl.multiple_of(side * half, half)
    send_ref[...] = jnp.dot(
        block, probes_ref[:, pl.ds(away, half)], preferred_element_type=jnp.float32
    )
    keep_ref[...] = jnp.dot(
        block, probes_ref[:, pl.ds(home, half)], preferred_element_type=jnp.float32
    )


def on_device(matrix, probes, leaf_skeleton, node_skeleton):
    n_grp = lax.axis_size("grp")
    n_leaf = lax.axis_size("leaf")
    grp_pos = lax.axis_index("grp")
    leaf_pos = lax.axis_index("leaf")
    device = grp_pos * n_leaf + leaf_pos
    side = leaf_pos & 1
    spot = leaf_pos >> 1
    spots = n_leaf // 2
    row_count, col_count = matrix.shape
    leaf_rows = row_count // n_leaf
    half = probes.shape[1] // 2
    rank = leaf_skeleton.shape[1]
    all_leaves = n_grp * n_leaf
    leaf_bits, grp_bits = bits_of(n_leaf), bits_of(n_grp)
    levels = leaf_bits + grp_bits

    def across(value, where=range(spots)):
        pairs = [(2 * z + s, 2 * z + 1 - s) for z in where for s in range(2)]
        return lax.ppermute(value, "leaf", pairs)

    def along(value, hops):
        pairs = [(2 * a + s, 2 * b + s) for a, b in hops for s in range(2)]
        return lax.ppermute(value, "leaf", pairs)

    def product(target):
        place = jnp.stack([target, grp_pos, leaf_pos]).astype(jnp.int32)
        out = jax.ShapeDtypeStruct((2 * leaf_rows, half), jnp.float32)
        return pl.pallas_call(
            lambda *refs: product_kernel(n_leaf, n_grp, *refs),
            out_shape=(out, out),
            grid_spec=pltpu.PrefetchScalarGridSpec(
                num_scalar_prefetch=1,
                grid=(2,),
                in_specs=[
                    pl.BlockSpec((leaf_rows, col_count), lambda i, at: (2 * at[0] + i, 0)),
                    pl.BlockSpec(probes.shape, lambda i, at: (0, 0)),
                ],
                out_specs=[
                    pl.BlockSpec((leaf_rows, half), lambda i, at: (i, 0)),
                    pl.BlockSpec((leaf_rows, half), lambda i, at: (i, 0)),
                ],
            ),
            name="product",
        )(place, matrix, probes)

    other_leaf = across(leaf_skeleton)

    def summed(target, where):
        send, keep = product(jnp.clip(target, 0, spots - 1))
        return keep + across(send, where)

    up = down = None
    for step in range(1, spots):
        ups = range(0, step)
        downs = range(spots - step, spots)
        up_target = spots - step + spot
        down_target = step - spots + spot
        if step <= spots // 2:
            mine = summed(
                jnp.where(spot < step, up_target, down_target), sorted({*ups, *downs})
            )
            mine_up = mine_down = mine
        else:
            mine_up = summed(up_target, ups)
            mine_down = summed(down_target, downs)
        if up is not None:
            mine_up = mine_up + up
            mine_down = mine_down + down
        up = along(mine_up, [(z, z + 1) for z in ups])
        down = along(mine_down, [(z, z - 1) for z in downs])
    samples = summed(spot, range(spots))
    if up is not None:
        samples = samples + up + down

    def cross_of(stacked, rows):
        return lax.dot_general(
            stacked, rows, (((1,), (1,)), ((), ())), precision=HIGHEST
        )

    first = jnp.where(side == 0, leaf_skeleton[0], other_leaf[0])
    second = jnp.where(side == 0, other_leaf[0], leaf_skeleton[0])
    stacks = (samples[:leaf_rows], samples[leaf_rows:])
    rows = tuple(jnp.take(z, j, axis=0) for z, j in zip(stacks, (first, second)))
    crosses = tuple(cross_of(z, r) for z, r in zip(stacks, rows))
    own = jnp.where(side == 0, crosses[0], crosses[1])
    received = across(jnp.where(side == 0, crosses[1], crosses[0]))
    leaf_basis = basis_of(own, received, leaf_skeleton[0])

    def level_offset(level):
        return sum(all_leaves >> inner for inner in range(1, level))

    def picked_of(level):
        node = level_offset(level) + (device >> level)
        return lax.dynamic_slice_in_dim(node_skeleton, node, 1, 0)[0]

    low_stack = jnp.concatenate(rows, axis=0)
    low_picked = picked_of(1)
    current = low_rows = jnp.take(low_stack, low_picked, axis=0)
    low_cross = cross_of(low_stack, low_rows)
    high_stack, high_picked, high_rows = low_stack, low_picked, low_rows
    even = device - side
    for level in range(2, levels + 1):
        if level <= leaf_bits:
            bit = level - 2
            hops = [(z, z ^ 1 << bit) for z in range(0, spots, 1 << bit)]
            partner = along(current, hops)
            upper = spot >> bit & 1
        else:
            bit = level - leaf_bits - 1
            pairs = [
                (g * n_leaf + s, (g ^ 1 << bit) * n_leaf + s)
                for g in range(0, n_grp, 1 << bit)
                for s in range(2)
            ]
            partner = lax.ppermute(current, ("grp", "leaf"), pairs)
            upper = grp_pos >> bit & 1
        stacked = jnp.concatenate(
            [
                jnp.where(upper == 1, partner, current),
                jnp.where(upper == 1, current, partner),
            ],
            axis=0,
        )
        picked = picked_of(level)
        current = jnp.take(stacked, picked, axis=0)
        select = even % (1 << level) == 1 << level - 1
        if level == levels:
            select = select | (even == 0)
        high_stack = jnp.where(select, stacked, high_stack)
        high_rows = jnp.where(select, current, high_rows)
        high_picked = jnp.where(select, picked, high_picked)
    high_cross = cross_of(high_stack, high_rows)
    own = jnp.where(side == 1, low_cross, high_cross)
    received = across(jnp.where(side == 1, high_cross, low_cross))
    node_picked = jnp.where(side == 1, low_picked, high_picked)
    transfer = basis_of(own, received, node_picked)
    return (leaf_basis, transfer[None])


def solution(mesh):
    return jax.shard_map(
        on_device,
        mesh=mesh,
        in_specs=(P("grp", "leaf"), P("leaf", None), P(("grp", "leaf"), None), P()),
        out_specs=(P(("grp", "leaf"), None), P(("grp", "leaf"), None, None)),
        check_vma=False,
    )
```

```python
import jax
import jax.numpy as jnp
from jax import lax
from jax.experimental import pallas as pl
from jax.experimental.pallas import tpu as pltpu
from jax.sharding import PartitionSpec as P


HIGHEST = lax.Precision.HIGHEST
GROUP = 1


def bits_of(count):
    return count.bit_length() - 1


def spd_inverse(a):
    n = a.shape[0]
    tiles = [a[8 * r : 8 * r + 8, :] for r in range(n // 8)]
    lane = lax.broadcasted_iota(jnp.int32, (8, n), 1)
    sub = lax.broadcasted_iota(jnp.int32, (8, n), 0)
    for kb in range(n // 8):
        k = 8 * kb
        edge = [jnp.broadcast_to(tiles[kb][:, k + j : k + j + 1], (8, n)) for j in range(8)]
        d = {
            (i, j): jnp.broadcast_to(edge[j][i : i + 1, :], (8, n))
            for i in range(8)
            for j in range(i + 1)
        }
        inside = (lane >= k) & (lane < k + 8)
        base = jnp.where(inside, jnp.where(lane - k == sub, 1.0, 0.0), tiles[kb])
        p = [jnp.broadcast_to(base[j : j + 1, :], (8, n)) for j in range(8)]
        inv, low = [None] * 8, {}
        for j in range(8):
            inv[j] = 1.0 / d[j, j]
            for i in range(j + 1, 8):
                low[i, j] = d[i, j] * inv[j]
            for i in range(j + 1, 8):
                for m in range(j + 1, i + 1):
                    d[i, m] = d[i, m] - low[i, j] * d[m, j]
                p[i] = p[i] - low[i, j] * p[j]
        w = [p[j] * inv[j] for j in range(8)]
        for j in range(7, 0, -1):
            for i in range(j):
                w[i] = w[i] - low[j, i] * w[j]
        fresh = []
        for r, t in enumerate(tiles):
            if r == kb:
                x = w[0]
                for j in range(1, 8):
                    x = jnp.where(sub == j, w[j], x)
            else:
                x = jnp.where(inside, 0.0, t)
                col = [jnp.broadcast_to(t[:, k + j : k + j + 1], (8, n)) for j in range(8)]
                pairs = [col[j] * w[j] + col[j + 1] * w[j + 1] for j in range(0, 8, 2)]
                x = x - ((pairs[0] + pairs[1]) + (pairs[2] + pairs[3]))
            fresh.append(x)
        tiles = fresh
    return jnp.concatenate(tiles, axis=0)


def dot(a, b, dims=((1,), (0,)), precision=HIGHEST):
    return lax.dot_general(
        a, b, (dims, ((), ())), precision=precision, preferred_element_type=jnp.float32
    )


def choices(picked, count):
    rank = picked.shape[1]
    index = lax.broadcasted_iota(jnp.int32, (count, rank), 0)
    chosen = index == picked
    ahead = jnp.sum((picked < index).astype(jnp.float32), axis=1, keepdims=True)
    member = jnp.sum(chosen.astype(jnp.float32), axis=1, keepdims=True)
    place = index.astype(jnp.float32) - ahead
    slot = lax.broadcasted_iota(jnp.int32, (count, rank), 1).astype(jnp.float32)
    others = (slot == place) & (jnp.broadcast_to(member, place.shape) < 0.5)
    return chosen.astype(jnp.float32), others.astype(jnp.float32)


def inverse_kernel(own_ref, received_ref, out_ref):
    out_ref[...] = spd_inverse(own_ref[...] + received_ref[...])


def leaf_kernel(own_ref, received_ref, inverse_ref, picked_ref, basis_ref):
    chosen, others = choices(picked_ref[...], basis_ref.shape[0])
    solved = dot(own_ref[...] + received_ref[...], inverse_ref[...])
    basis_ref[...] = chosen + dot(others, solved)


def node_kernel(own_ref, received_ref, picked_ref, basis_ref):
    cross = own_ref[...] + received_ref[...]
    index = lax.broadcasted_iota(jnp.int32, cross.shape, 0)
    choice = (index == picked_ref[...]).astype(jnp.float32)
    gram = dot(choice, cross, ((0,), (0,)))
    basis_ref[...] = dot(cross, spd_inverse(gram))


def unit_rows(matrix_ref, hit, n_grp):
    rows = matrix_ref.shape[0]
    pieces = []
    for c in range(n_grp):
        piece = matrix_ref[:, c * rows : (c + 1) * rows]
        pieces.append(jnp.where(hit == c, jnp.zeros_like(piece), piece))
    return pieces


def sides(block, probes_ref, side, half):
    away = probes_ref[:, pl.ds(pl.multiple_of((1 - side) * half, half), half)]
    home = probes_ref[:, pl.ds(pl.multiple_of(side * half, half), half)]
    return dot(block, away, precision=None), dot(block, home, precision=None)


def plain_kernel(n_leaf, n_grp, mask, place_ref, matrix_ref, probes_ref, send_ref, keep_ref):
    spot = (place_ref[1] >> 1) ^ mask
    hit = place_ref[0] * n_leaf + 2 * spot + pl.program_id(0) - place_ref[1] * n_grp
    block = jnp.concatenate(unit_rows(matrix_ref, hit, n_grp), axis=1)
    send_ref[...], keep_ref[...] = sides(block, probes_ref, place_ref[1] & 1, send_ref.shape[1])


def ordered_kernel(n_leaf, n_grp, high, place_ref, matrix_ref, probes_ref, picked_ref, *outs):
    step = pl.program_id(0)
    spot = (place_ref[1] >> 1) ^ (high - step // 2)
    hit = place_ref[0] * n_leaf + 2 * spot + step % 2 - place_ref[1] * n_grp
    rank, half = picked_ref.shape[2], outs[0].shape[1]
    chosen, others = choices(picked_ref[0], matrix_ref.shape[0])
    order = jnp.concatenate([chosen, others], axis=1).astype(jnp.bfloat16)
    block = jnp.concatenate(
        [
            dot(order, piece, ((0,), (0,)), None).astype(jnp.bfloat16)
            for piece in unit_rows(matrix_ref, hit, n_grp)
        ],
        axis=1,
    )
    away, home = sides(block, probes_ref, place_ref[1] & 1, half)
    for j in range(len(outs) // 4):

        @pl.when(step // 2 == j)
        def _():
            at = pl.ds(pl.multiple_of(step % 2 * rank, rank), rank)
            outs[4 * j][at, :] = away[:rank]
            outs[4 * j + 1][at, :] = home[:rank]
            outs[4 * j + 2][at, :] = away[rank:]
            outs[4 * j + 3][at, :] = home[rank:]


def split_kernel(place_ref, keep_ref, received_ref, picked_ref, first_ref, second_ref):
    total = keep_ref[...] + received_ref[...]
    chosen, others = choices(picked_ref[0], total.shape[0])
    first_ref[...] = dot(chosen, total, ((0,), (0,)))
    second_ref[...] = dot(others, total, ((0,), (0,)))


def on_device(matrix, probes, leaf_skeleton, node_skeleton):
    n_grp = lax.axis_size("grp")
    n_leaf = lax.axis_size("leaf")
    grp_pos = lax.axis_index("grp")
    leaf_pos = lax.axis_index("leaf")
    device = grp_pos * n_leaf + leaf_pos
    side = leaf_pos & 1
    spot = leaf_pos >> 1
    spots = n_leaf // 2
    row_count, col_count = matrix.shape
    leaf_rows = row_count // n_leaf
    half = probes.shape[1] // 2
    rank = leaf_skeleton.shape[1]
    all_leaves = n_grp * n_leaf
    leaf_bits, grp_bits = bits_of(n_leaf), bits_of(n_grp)
    levels = leaf_bits + grp_bits

    def across(value):
        return lax.ppermute(value, "leaf", [(p, p ^ 1) for p in range(n_leaf)])

    def along(value, hops):
        pairs = [(2 * a + s, 2 * b + s) for a, b in hops for s in range(2)]
        return lax.ppermute(value, "leaf", pairs)

    place = jnp.stack([grp_pos, leaf_pos]).astype(jnp.int32)
    masks = list(range(spots - 1, -1, -1))
    top = masks[0]
    wide = jax.ShapeDtypeStruct((2 * leaf_rows, half), jnp.float32)
    slim = jax.ShapeDtypeStruct((2 * rank, half), jnp.float32)

    def leaf_row(high):
        return lambda i, at: 2 * ((at[1] >> 1) ^ (high - i // 2)) + i % 2

    def grid_spec(count, in_specs, out_specs):
        return pltpu.PrefetchScalarGridSpec(
            num_scalar_prefetch=1, grid=(count,), in_specs=in_specs, out_specs=out_specs
        )

    def matrix_specs(high):
        row = leaf_row(high)
        return [
            pl.BlockSpec((leaf_rows, col_count), lambda i, at: (row(i, at), 0)),
            pl.BlockSpec(probes.shape, lambda i, at: (0, 0)),
        ]

    def picked_spec(high):
        row = leaf_row(high)
        return pl.BlockSpec((1, 1, rank), lambda i, at: (row(i, at), 0, 0))

    send, keep = pl.pallas_call(
        lambda *refs: plain_kernel(n_leaf, n_grp, top, *refs),
        out_shape=(wide,) * 2,
        grid_spec=grid_spec(
            2, matrix_specs(top), [pl.BlockSpec((leaf_rows, half), lambda i, at: (i, 0))] * 2
        ),
        name="product",
    )(place, matrix, probes)

    skeletons = leaf_skeleton
    for bit in range(leaf_bits):
        partner = lax.ppermute(skeletons, "leaf", [(p, p ^ 1 << bit) for p in range(n_leaf)])
        if bit == 0:
            send, partner = lax.optimization_barrier((send, partner))
        skeletons = jnp.where(
            leaf_pos >> bit & 1 == 1,
            jnp.concatenate([partner, skeletons], axis=0),
            jnp.concatenate([skeletons, partner], axis=0),
        )
    top_received = across(send)
    tables = skeletons[:, None, :]

    def ordered(group):
        high, count = group[0], len(group)
        outs = pl.pallas_call(
            lambda *refs: ordered_kernel(n_leaf, n_grp, high, *refs),
            out_shape=(slim,) * (4 * count),
            grid_spec=grid_spec(
                2 * count,
                [*matrix_specs(high), picked_spec(high)],
                [pl.BlockSpec(slim.shape, lambda i, at: (0, 0))] * (4 * count),
            ),
            name="ordered",
        )
        outs = outs(place, matrix, probes, tables)
        return {mask: outs[4 * j : 4 * j + 4] for j, mask in enumerate(group)}

    pieces = {}
    for at in range(1, spots, GROUP):
        pieces.update(ordered(masks[at : at + GROUP]))

    piece = pl.BlockSpec((leaf_rows, half), lambda i, at: (i, 0))
    part = pl.BlockSpec((rank, half), lambda i, at: (i, 0))
    first, second = {}, {}
    first[top], second[top] = pl.pallas_call(
        split_kernel,
        out_shape=(slim,) * 2,
        grid_spec=grid_spec(2, [piece, piece, picked_spec(top)], [part] * 2),
        name="split",
    )(place, keep, top_received, tables)

    for mask in masks[1:]:
        received = across(pieces[mask][0])
        first[mask] = pieces[mask][1] + received
        if mask == min(1, top):
            gate = received
    for mask in masks[1:]:
        send, _ = lax.optimization_barrier((pieces[mask][2], gate))
        second[mask] = pieces[mask][3] + across(send)

    def gathered(values, gates=None):
        values = dict(values)
        for mask in masks[:-1]:
            bit = mask & -mask
            value = values[mask]
            if gates is not None:
                gate = gates[0] if mask == top else gates[1]
                value, _ = lax.optimization_barrier((value, gate))
            elif mask ^ bit == 0:
                early.append(value)
            arrived = along(value, [(z, z ^ bit) for z in range(spots)])
            if gates is not None and mask != top:
                arrived, _ = lax.optimization_barrier((arrived, gates[2]))
            values[mask ^ bit] = values[mask ^ bit] + arrived
        return values[0]

    early = []

    skeleton_rows = gathered(first)

    def cross_of(stacked, rows):
        return dot(stacked, rows, ((1,), (1,)))

    halves = (skeleton_rows[:rank], skeleton_rows[rank:])
    grams = [cross_of(r, r) for r in halves]
    own_gram = jnp.where(side == 0, grams[0], grams[1])
    received_gram = across(jnp.where(side == 0, grams[1], grams[0]))

    def level_offset(level):
        return sum(all_leaves >> inner for inner in range(1, level))

    def picked_of(level):
        node = level_offset(level) + (device >> level)
        return lax.dynamic_slice_in_dim(node_skeleton, node, 1, 0)[0]

    gates = []
    low_stack = skeleton_rows
    low_picked = picked_of(1)
    current = low_rows = jnp.take(low_stack, low_picked, axis=0)
    low_cross = cross_of(low_stack, low_rows)
    high_stack, high_picked, high_rows = low_stack, low_picked, low_rows
    even = device - side
    for level in range(2, levels + 1):
        if level <= leaf_bits:
            bit = level - 2
            hops = [(z, z ^ 1 << bit) for z in range(0, spots, 1 << bit)]
            partner = along(current, hops)
            upper = spot >> bit & 1
            gates.append(partner)
        else:
            bit = level - leaf_bits - 1
            pairs = [
                (g * n_leaf + s, (g ^ 1 << bit) * n_leaf + s)
                for g in range(0, n_grp, 1 << bit)
                for s in range(2)
            ]
            partner = lax.ppermute(current, ("grp", "leaf"), pairs)
            upper = grp_pos >> bit & 1
        stacked = jnp.concatenate(
            [
                jnp.where(upper == 1, partner, current),
                jnp.where(upper == 1, current, partner),
            ],
            axis=0,
        )
        picked = picked_of(level)
        current = jnp.take(stacked, picked, axis=0)
        select = even % (1 << level) == 1 << level - 1
        if level == levels:
            select = select | (even == 0)
        high_stack = jnp.where(select, stacked, high_stack)
        high_rows = jnp.where(select, current, high_rows)
        high_picked = jnp.where(select, picked, high_picked)
    high_cross = cross_of(high_stack, high_rows)
    own = jnp.where(side == 1, low_cross, high_cross)
    sent = jnp.where(side == 1, high_cross, low_cross)
    received = across(sent)
    own_gram, _ = lax.optimization_barrier((own_gram, sent))
    square = jax.ShapeDtypeStruct((rank, rank), jnp.float32)
    inverse = pl.pallas_call(inverse_kernel, out_shape=square, name="inverse")(own_gram, received_gram)
    node_picked = jnp.where(side == 1, low_picked, high_picked)
    other_rows = gathered(second, [early[0], gates[-1], inverse])
    crosses = [
        cross_of(z, r) for z, r in zip((other_rows[:rank], other_rows[rank:]), halves)
    ]
    own_leaf = jnp.where(side == 0, crosses[0], crosses[1])
    received_leaf = across(jnp.where(side == 0, crosses[1], crosses[0]))
    tall = jax.ShapeDtypeStruct((leaf_rows, rank), jnp.float32)
    leaf_basis = pl.pallas_call(leaf_kernel, out_shape=tall, name="leaf_basis")(
        own_leaf, received_leaf, inverse, leaf_skeleton
    )

    received, *_ = lax.optimization_barrier((received, *crosses))
    tall = jax.ShapeDtypeStruct((2 * rank, rank), jnp.float32)
    transfer = pl.pallas_call(node_kernel, out_shape=tall, name="node_basis")(
        own, received, node_picked[None]
    )
    return (leaf_basis, transfer[None])


def solution(mesh):
    return jax.shard_map(
        on_device,
        mesh=mesh,
        in_specs=(P("grp", "leaf"), P("leaf", None), P(("grp", "leaf"), None), P()),
        out_specs=(P(("grp", "leaf"), None), P(("grp", "leaf"), None, None)),
        check_vma=False,
    )
```

```python
import jax
import jax.numpy as jnp
from jax import lax
from jax.experimental import pallas as pl
from jax.experimental.pallas import tpu as pltpu
from jax.sharding import PartitionSpec as P


HIGHEST = lax.Precision.HIGHEST
GROUP = 1


def bits_of(count):
    return count.bit_length() - 1


def spd_inverse(a):
    n = a.shape[0]
    tiles = [a[8 * r : 8 * r + 8, :] for r in range(n // 8)]
    lane = lax.broadcasted_iota(jnp.int32, (8, n), 1)
    sub = lax.broadcasted_iota(jnp.int32, (8, n), 0)
    for kb in range(n // 8):
        k = 8 * kb
        edge = [jnp.broadcast_to(tiles[kb][:, k + j : k + j + 1], (8, n)) for j in range(8)]
        d = {
            (i, j): jnp.broadcast_to(edge[j][i : i + 1, :], (8, n))
            for i in range(8)
            for j in range(i + 1)
        }
        inside = (lane >= k) & (lane < k + 8)
        base = jnp.where(inside, jnp.where(lane - k == sub, 1.0, 0.0), tiles[kb])
        p = [jnp.broadcast_to(base[j : j + 1, :], (8, n)) for j in range(8)]
        inv, low = [None] * 8, {}
        for j in range(8):
            inv[j] = 1.0 / d[j, j]
            for i in range(j + 1, 8):
                low[i, j] = d[i, j] * inv[j]
            for i in range(j + 1, 8):
                for m in range(j + 1, i + 1):
                    d[i, m] = d[i, m] - low[i, j] * d[m, j]
                p[i] = p[i] - low[i, j] * p[j]
        w = [p[j] * inv[j] for j in range(8)]
        for j in range(7, 0, -1):
            for i in range(j):
                w[i] = w[i] - low[j, i] * w[j]
        fresh = []
        for r, t in enumerate(tiles):
            if r == kb:
                x = w[0]
                for j in range(1, 8):
                    x = jnp.where(sub == j, w[j], x)
            else:
                x = jnp.where(inside, 0.0, t)
                col = [jnp.broadcast_to(t[:, k + j : k + j + 1], (8, n)) for j in range(8)]
                pairs = [col[j] * w[j] + col[j + 1] * w[j + 1] for j in range(0, 8, 2)]
                x = x - ((pairs[0] + pairs[1]) + (pairs[2] + pairs[3]))
            fresh.append(x)
        tiles = fresh
    return jnp.concatenate(tiles, axis=0)


def dot(a, b, dims=((1,), (0,)), precision=HIGHEST):
    return lax.dot_general(
        a, b, (dims, ((), ())), precision=precision, preferred_element_type=jnp.float32
    )


def choices(picked, count):
    rank = picked.shape[1]
    index = lax.broadcasted_iota(jnp.int32, (count, rank), 0)
    chosen = index == picked
    ahead = jnp.sum((picked < index).astype(jnp.float32), axis=1, keepdims=True)
    member = jnp.sum(chosen.astype(jnp.float32), axis=1, keepdims=True)
    place = index.astype(jnp.float32) - ahead
    slot = lax.broadcasted_iota(jnp.int32, (count, rank), 1).astype(jnp.float32)
    others = (slot == place) & (jnp.broadcast_to(member, place.shape) < 0.5)
    return chosen.astype(jnp.float32), others.astype(jnp.float32)


def inverse_kernel(own_ref, received_ref, out_ref):
    out_ref[...] = spd_inverse(own_ref[...] + received_ref[...])


def finish_kernel(
    node_at, own_ref, received_ref, inverse_ref, picked_ref, table_ref, leaf_ref, node_ref
):
    total = own_ref[...] + received_ref[...]
    rank = total.shape[1]
    cross = total[rank:]
    index = lax.broadcasted_iota(jnp.int32, cross.shape, 0)
    choice = (index == table_ref[pl.ds(node_at[0], 1), :]).astype(jnp.float32)
    gram = dot(choice, cross, ((0,), (0,)))
    chosen, others = choices(picked_ref[...], leaf_ref.shape[0])
    leaf_ref[...] = chosen + dot(others, dot(total[:rank], inverse_ref[...]))
    node_ref[...] = dot(cross, spd_inverse(gram))


def unit_rows(matrix_ref, hit, n_grp):
    rows = matrix_ref.shape[0]
    pieces = []
    for c in range(n_grp):
        piece = matrix_ref[:, c * rows : (c + 1) * rows]
        pieces.append(jnp.where(hit == c, jnp.zeros_like(piece), piece))
    return pieces


def sides(block, probes_ref, side, half):
    away = probes_ref[:, pl.ds(pl.multiple_of((1 - side) * half, half), half)]
    home = probes_ref[:, pl.ds(pl.multiple_of(side * half, half), half)]
    return dot(block, away, precision=None), dot(block, home, precision=None)


def plain_kernel(n_leaf, n_grp, mask, place_ref, matrix_ref, probes_ref, send_ref, keep_ref):
    spot = (place_ref[1] >> 1) ^ mask
    hit = place_ref[0] * n_leaf + 2 * spot + pl.program_id(0) - place_ref[1] * n_grp
    block = jnp.concatenate(unit_rows(matrix_ref, hit, n_grp), axis=1)
    send_ref[...], keep_ref[...] = sides(block, probes_ref, place_ref[1] & 1, send_ref.shape[1])


def ordered_kernel(n_leaf, n_grp, high, place_ref, matrix_ref, probes_ref, picked_ref, *outs):
    step = pl.program_id(0)
    spot = (place_ref[1] >> 1) ^ (high - step // 2)
    hit = place_ref[0] * n_leaf + 2 * spot + step % 2 - place_ref[1] * n_grp
    rank, half = picked_ref.shape[2], outs[0].shape[1]
    chosen, others = choices(picked_ref[0], matrix_ref.shape[0])
    order = jnp.concatenate([chosen, others], axis=1).astype(jnp.bfloat16)
    block = jnp.concatenate(
        [
            dot(order, piece, ((0,), (0,)), None).astype(jnp.bfloat16)
            for piece in unit_rows(matrix_ref, hit, n_grp)
        ],
        axis=1,
    )
    away, home = sides(block, probes_ref, place_ref[1] & 1, half)
    for j in range(len(outs) // 4):

        @pl.when(step // 2 == j)
        def _():
            at = pl.ds(pl.multiple_of(step % 2 * rank, rank), rank)
            outs[4 * j][at, :] = away[:rank]
            outs[4 * j + 1][at, :] = home[:rank]
            outs[4 * j + 2][at, :] = away[rank:]
            outs[4 * j + 3][at, :] = home[rank:]


def split_kernel(place_ref, keep_ref, received_ref, picked_ref, first_ref, second_ref):
    total = keep_ref[...] + received_ref[...]
    chosen, others = choices(picked_ref[0], total.shape[0])
    first_ref[...] = dot(chosen, total, ((0,), (0,)))
    second_ref[...] = dot(others, total, ((0,), (0,)))


def on_device(matrix, probes, leaf_skeleton, node_skeleton):
    n_grp = lax.axis_size("grp")
    n_leaf = lax.axis_size("leaf")
    grp_pos = lax.axis_index("grp")
    leaf_pos = lax.axis_index("leaf")
    device = grp_pos * n_leaf + leaf_pos
    side = leaf_pos & 1
    spot = leaf_pos >> 1
    spots = n_leaf // 2
    row_count, col_count = matrix.shape
    leaf_rows = row_count // n_leaf
    half = probes.shape[1] // 2
    rank = leaf_skeleton.shape[1]
    all_leaves = n_grp * n_leaf
    leaf_bits, grp_bits = bits_of(n_leaf), bits_of(n_grp)
    levels = leaf_bits + grp_bits

    def across(value):
        return lax.ppermute(value, "leaf", [(p, p ^ 1) for p in range(n_leaf)])

    def along(value, hops):
        pairs = [(2 * a + s, 2 * b + s) for a, b in hops for s in range(2)]
        return lax.ppermute(value, "leaf", pairs)

    place = jnp.stack([grp_pos, leaf_pos]).astype(jnp.int32)
    masks = list(range(spots - 1, -1, -1))
    top = masks[0]
    wide = jax.ShapeDtypeStruct((2 * leaf_rows, half), jnp.float32)
    slim = jax.ShapeDtypeStruct((2 * rank, half), jnp.float32)

    def leaf_row(high):
        return lambda i, at: 2 * ((at[1] >> 1) ^ (high - i // 2)) + i % 2

    def grid_spec(count, in_specs, out_specs):
        return pltpu.PrefetchScalarGridSpec(
            num_scalar_prefetch=1, grid=(count,), in_specs=in_specs, out_specs=out_specs
        )

    def matrix_specs(high):
        row = leaf_row(high)
        return [
            pl.BlockSpec((leaf_rows, col_count), lambda i, at: (row(i, at), 0)),
            pl.BlockSpec(probes.shape, lambda i, at: (0, 0)),
        ]

    def picked_spec(high):
        row = leaf_row(high)
        return pl.BlockSpec((1, 1, rank), lambda i, at: (row(i, at), 0, 0))

    send, keep = pl.pallas_call(
        lambda *refs: plain_kernel(n_leaf, n_grp, top, *refs),
        out_shape=(wide,) * 2,
        grid_spec=grid_spec(
            2, matrix_specs(top), [pl.BlockSpec((leaf_rows, half), lambda i, at: (i, 0))] * 2
        ),
        name="product",
    )(place, matrix, probes)

    skeletons = leaf_skeleton
    for bit in range(leaf_bits):
        partner = lax.ppermute(skeletons, "leaf", [(p, p ^ 1 << bit) for p in range(n_leaf)])
        if bit == 0:
            send, partner = lax.optimization_barrier((send, partner))
        skeletons = jnp.where(
            leaf_pos >> bit & 1 == 1,
            jnp.concatenate([partner, skeletons], axis=0),
            jnp.concatenate([skeletons, partner], axis=0),
        )
    top_received = across(send)
    tables = skeletons[:, None, :]

    def ordered(group):
        high, count = group[0], len(group)
        outs = pl.pallas_call(
            lambda *refs: ordered_kernel(n_leaf, n_grp, high, *refs),
            out_shape=(slim,) * (4 * count),
            grid_spec=grid_spec(
                2 * count,
                [*matrix_specs(high), picked_spec(high)],
                [pl.BlockSpec(slim.shape, lambda i, at: (0, 0))] * (4 * count),
            ),
            name="ordered",
        )
        outs = outs(place, matrix, probes, tables)
        return {mask: outs[4 * j : 4 * j + 4] for j, mask in enumerate(group)}

    pieces = {}
    for at in range(1, spots, GROUP):
        pieces.update(ordered(masks[at : at + GROUP]))

    piece = pl.BlockSpec((leaf_rows, half), lambda i, at: (i, 0))
    part = pl.BlockSpec((rank, half), lambda i, at: (i, 0))
    first, second = {}, {}
    split = pl.pallas_call(
        split_kernel,
        out_shape=(slim,) * 2,
        grid_spec=grid_spec(2, [piece, piece, picked_spec(top)], [part] * 2),
        name="split",
    )
    first[top], second[top] = split(place, keep, top_received, tables)

    for mask in masks[1:]:
        received = across(pieces[mask][0])
        first[mask] = pieces[mask][1] + received
        if mask == min(1, top):
            gate = received
    for mask in masks[1:]:
        send, _ = lax.optimization_barrier((pieces[mask][2], gate))
        second[mask] = pieces[mask][3] + across(send)

    def gathered(values, gates=None):
        values = dict(values)
        for mask in masks[:-1]:
            bit = mask & -mask
            value = values[mask]
            if gates is not None:
                gate = gates[0] if mask == top else gates[1]
                value, _ = lax.optimization_barrier((value, gate))
            elif mask ^ bit == 0:
                early.append(value)
            arrived = along(
                value, [(z, z ^ bit) for z in range(spots)]
            )
            if gates is not None and mask != top:
                arrived, _ = lax.optimization_barrier((arrived, gates[2]))
            values[mask ^ bit] = values[mask ^ bit] + arrived
        return values[0]

    early = []

    skeleton_rows = gathered(first)

    def cross_of(stacked, rows):
        return dot(stacked, rows, ((1,), (1,)))

    halves = (skeleton_rows[:rank], skeleton_rows[rank:])
    grams = [cross_of(r, r) for r in halves]
    own_gram = jnp.where(side == 0, grams[0], grams[1])
    received_gram = across(jnp.where(side == 0, grams[1], grams[0]))

    def level_offset(level):
        return sum(all_leaves >> inner for inner in range(1, level))

    def picked_of(level):
        node = level_offset(level) + (device >> level)
        return lax.dynamic_slice_in_dim(node_skeleton, node, 1, 0)[0]

    gates = []
    low_stack = skeleton_rows
    low_picked = picked_of(1)
    node_own = device >> 1
    current = jnp.take(low_stack, low_picked, axis=0)
    low_cross = high_cross = cross_of(low_stack, current)
    even = device - side
    for level in range(2, levels + 1):
        if level <= leaf_bits:
            bit = level - 2
            hops = [(z, z ^ 1 << bit) for z in range(0, spots, 1 << bit)]
            partner = along(current, hops)
            upper = spot >> bit & 1
            gates.append(partner)
        else:
            bit = level - leaf_bits - 1
            pairs = [
                (g * n_leaf + s, (g ^ 1 << bit) * n_leaf + s)
                for g in range(0, n_grp, 1 << bit)
                for s in range(2)
            ]
            send = lambda value: lax.ppermute(value, ("grp", "leaf"), pairs)
            partner = send(current)
            upper = grp_pos >> bit & 1
        stacked = jnp.concatenate(
            [
                jnp.where(upper == 1, partner, current),
                jnp.where(upper == 1, current, partner),
            ],
            axis=0,
        )
        picked = picked_of(level)
        current = jnp.take(stacked, picked, axis=0)
        select = even % (1 << level) == 1 << level - 1
        if level == levels:
            select = select | (even == 0)
        high_cross = jnp.where(select, cross_of(stacked, current), high_cross)
        node = level_offset(level) + (device >> level)
        node_own = jnp.where(select & (side == 0), node, node_own)

    other_rows = gathered(second, [early[0], gates[0], current])
    crosses = [
        cross_of(z, r) for z, r in zip((other_rows[:rank], other_rows[rank:]), halves)
    ]
    own = jnp.concatenate(
        [
            jnp.where(side == 0, crosses[0], crosses[1]),
            jnp.where(side == 1, low_cross, high_cross),
        ],
        axis=0,
    )
    sent = jnp.concatenate(
        [
            jnp.where(side == 0, crosses[1], crosses[0]),
            jnp.where(side == 1, high_cross, low_cross),
        ],
        axis=0,
    )
    received = across(sent)
    square = jax.ShapeDtypeStruct((rank, rank), jnp.float32)
    inverse = pl.pallas_call(inverse_kernel, out_shape=square, name="inverse")(own_gram, received_gram)
    tall = [jax.ShapeDtypeStruct((rows, rank), jnp.float32) for rows in (leaf_rows, 2 * rank)]
    whole = pl.BlockSpec(memory_space=pltpu.VMEM)
    leaf_basis, transfer = pl.pallas_call(
        finish_kernel,
        out_shape=tall,
        in_specs=[pl.BlockSpec(memory_space=pltpu.SMEM)] + [whole] * 5,
        name="finish",
    )(node_own[None], own, received, inverse, leaf_skeleton, node_skeleton)
    return (leaf_basis, transfer[None])


def solution(mesh):
    return jax.shard_map(
        on_device,
        mesh=mesh,
        in_specs=(P("grp", "leaf"), P("leaf", None), P(("grp", "leaf"), None), P()),
        out_specs=(P(("grp", "leaf"), None), P(("grp", "leaf"), None, None)),
        check_vma=False,
    )
```

```python
import jax
import jax.numpy as jnp
from jax import lax
from jax.experimental import pallas as pl
from jax.experimental.pallas import tpu as pltpu
from jax.sharding import PartitionSpec as P


HIGHEST = lax.Precision.HIGHEST
GROUP = 1


def bits_of(count):
    return count.bit_length() - 1


def spd_inverse(a):
    n = a.shape[0]
    tiles = [a[8 * r : 8 * r + 8, :] for r in range(n // 8)]
    lane = lax.broadcasted_iota(jnp.int32, (8, n), 1)
    sub = lax.broadcasted_iota(jnp.int32, (8, n), 0)
    for kb in range(n // 8):
        k = 8 * kb
        edge = [jnp.broadcast_to(tiles[kb][:, k + j : k + j + 1], (8, n)) for j in range(8)]
        d = {
            (i, j): jnp.broadcast_to(edge[j][i : i + 1, :], (8, n))
            for i in range(8)
            for j in range(i + 1)
        }
        inside = (lane >= k) & (lane < k + 8)
        base = jnp.where(inside, jnp.where(lane - k == sub, 1.0, 0.0), tiles[kb])
        p = [jnp.broadcast_to(base[j : j + 1, :], (8, n)) for j in range(8)]
        inv, low = [None] * 8, {}
        for j in range(8):
            inv[j] = 1.0 / d[j, j]
            for i in range(j + 1, 8):
                low[i, j] = d[i, j] * inv[j]
            for i in range(j + 1, 8):
                for m in range(j + 1, i + 1):
                    d[i, m] = d[i, m] - low[i, j] * d[m, j]
                p[i] = p[i] - low[i, j] * p[j]
        w = [p[j] * inv[j] for j in range(8)]
        for j in range(7, 0, -1):
            for i in range(j):
                w[i] = w[i] - low[j, i] * w[j]
        fresh = []
        for r, t in enumerate(tiles):
            if r == kb:
                x = w[0]
                for j in range(1, 8):
                    x = jnp.where(sub == j, w[j], x)
            else:
                x = jnp.where(inside, 0.0, t)
                col = [jnp.broadcast_to(t[:, k + j : k + j + 1], (8, n)) for j in range(8)]
                pairs = [col[j] * w[j] + col[j + 1] * w[j + 1] for j in range(0, 8, 2)]
                x = x - ((pairs[0] + pairs[1]) + (pairs[2] + pairs[3]))
            fresh.append(x)
        tiles = fresh
    return jnp.concatenate(tiles, axis=0)


def dot(a, b, dims=((1,), (0,)), precision=HIGHEST):
    return lax.dot_general(
        a, b, (dims, ((), ())), precision=precision, preferred_element_type=jnp.float32
    )


def choices(picked, count):
    rank = picked.shape[1]
    index = lax.broadcasted_iota(jnp.int32, (count, rank), 0)
    chosen = index == picked
    ahead = jnp.sum((picked < index).astype(jnp.float32), axis=1, keepdims=True)
    member = jnp.sum(chosen.astype(jnp.float32), axis=1, keepdims=True)
    place = index.astype(jnp.float32) - ahead
    slot = lax.broadcasted_iota(jnp.int32, (count, rank), 1).astype(jnp.float32)
    others = (slot == place) & (jnp.broadcast_to(member, place.shape) < 0.5)
    return chosen.astype(jnp.float32), others.astype(jnp.float32)


def inverse_kernel(own_ref, received_ref, out_ref):
    out_ref[...] = spd_inverse(own_ref[...] + received_ref[...])


def finish_kernel(
    node_at, own_ref, received_ref, inverse_ref, picked_ref, table_ref, leaf_ref, node_ref
):
    total = own_ref[...] + received_ref[...]
    rank = total.shape[1]
    cross = total[rank:]
    index = lax.broadcasted_iota(jnp.int32, cross.shape, 0)
    choice = (index == table_ref[pl.ds(node_at[0], 1), :]).astype(jnp.float32)
    gram = dot(choice, cross, ((0,), (0,)))
    chosen, others = choices(picked_ref[...], leaf_ref.shape[0])
    leaf_ref[...] = chosen + dot(others, dot(total[:rank], inverse_ref[...]))
    node_ref[...] = dot(cross, spd_inverse(gram))


def unit_rows(matrix_ref, hit, n_grp):
    rows = matrix_ref.shape[0]
    pieces = []
    for c in range(n_grp):
        piece = matrix_ref[:, c * rows : (c + 1) * rows]
        pieces.append(jnp.where(hit == c, jnp.zeros_like(piece), piece))
    return pieces


def sides(block, probes_ref, side, half):
    away = probes_ref[:, pl.ds(pl.multiple_of((1 - side) * half, half), half)]
    home = probes_ref[:, pl.ds(pl.multiple_of(side * half, half), half)]
    return dot(block, away, precision=None), dot(block, home, precision=None)


def plain_kernel(n_leaf, n_grp, mask, matrix_ref, probes_ref, send_ref, keep_ref):
    spot = (lax.axis_index("leaf") >> 1) ^ mask
    hit = lax.axis_index("grp") * n_leaf + 2 * spot + pl.program_id(0) - lax.axis_index("leaf") * n_grp
    block = jnp.concatenate(unit_rows(matrix_ref, hit, n_grp), axis=1)
    send_ref[...], keep_ref[...] = sides(block, probes_ref, lax.axis_index("leaf") & 1, send_ref.shape[1])


def ordered_kernel(n_leaf, n_grp, high, matrix_ref, probes_ref, picked_ref, *outs):
    step = pl.program_id(0)
    spot = (lax.axis_index("leaf") >> 1) ^ (high - step // 2)
    hit = lax.axis_index("grp") * n_leaf + 2 * spot + step % 2 - lax.axis_index("leaf") * n_grp
    rank, half = picked_ref.shape[2], outs[0].shape[1]
    chosen, others = choices(picked_ref[0], matrix_ref.shape[0])
    order = jnp.concatenate([chosen, others], axis=1).astype(jnp.bfloat16)
    block = jnp.concatenate(
        [
            dot(order, piece, ((0,), (0,)), None).astype(jnp.bfloat16)
            for piece in unit_rows(matrix_ref, hit, n_grp)
        ],
        axis=1,
    )
    away, home = sides(block, probes_ref, lax.axis_index("leaf") & 1, half)
    for j in range(len(outs) // 4):

        @pl.when(step // 2 == j)
        def _():
            at = pl.ds(pl.multiple_of(step % 2 * rank, rank), rank)
            outs[4 * j][at, :] = away[:rank]
            outs[4 * j + 1][at, :] = home[:rank]
            outs[4 * j + 2][at, :] = away[rank:]
            outs[4 * j + 3][at, :] = home[rank:]


def split_kernel(keep_ref, received_ref, picked_ref, first_ref, second_ref):
    total = keep_ref[...] + received_ref[...]
    order = jnp.concatenate(choices(picked_ref[0], total.shape[0]), axis=1).astype(jnp.bfloat16)
    moved = None
    for _ in range(3):
        part = total.astype(jnp.bfloat16)
        total = total - part.astype(jnp.float32)
        value = dot(order, part, ((0,), (0,)), None)
        moved = value if moved is None else moved + value
    rank = first_ref.shape[0]
    first_ref[...] = moved[:rank]
    second_ref[...] = moved[rank:]


def on_device(matrix, probes, leaf_skeleton, node_skeleton):
    n_grp = lax.axis_size("grp")
    n_leaf = lax.axis_size("leaf")
    grp_pos = lax.axis_index("grp")
    leaf_pos = lax.axis_index("leaf")
    device = grp_pos * n_leaf + leaf_pos
    side = leaf_pos & 1
    spot = leaf_pos >> 1
    spots = n_leaf // 2
    row_count, col_count = matrix.shape
    leaf_rows = row_count // n_leaf
    half = probes.shape[1] // 2
    rank = leaf_skeleton.shape[1]
    all_leaves = n_grp * n_leaf
    leaf_bits, grp_bits = bits_of(n_leaf), bits_of(n_grp)
    levels = leaf_bits + grp_bits

    def across(value):
        return lax.ppermute(value, "leaf", [(p, p ^ 1) for p in range(n_leaf)])

    def along(value, hops):
        pairs = [(2 * a + s, 2 * b + s) for a, b in hops for s in range(2)]
        return lax.ppermute(value, "leaf", pairs)

    masks = list(range(spots - 1, -1, -1))
    top = masks[0]
    wide = jax.ShapeDtypeStruct((2 * leaf_rows, half), jnp.float32)
    slim = jax.ShapeDtypeStruct((2 * rank, half), jnp.float32)

    def leaf_row(high):
        return lambda i: 2 * ((lax.axis_index("leaf") >> 1) ^ (high - i // 2)) + i % 2

    def grid_spec(count, in_specs, out_specs):
        return pl.GridSpec(grid=(count,), in_specs=in_specs, out_specs=out_specs)

    def matrix_specs(high):
        row = leaf_row(high)
        return [
            pl.BlockSpec((leaf_rows, col_count), lambda i: (row(i), 0)),
            pl.BlockSpec(memory_space=pltpu.VMEM),
        ]

    def picked_spec(high):
        row = leaf_row(high)
        return pl.BlockSpec((1, 1, rank), lambda i: (row(i), 0, 0))

    send, keep = pl.pallas_call(
        lambda *refs: plain_kernel(n_leaf, n_grp, top, *refs),
        out_shape=(wide,) * 2,
        grid_spec=grid_spec(
            2, matrix_specs(top), [pl.BlockSpec((leaf_rows, half), lambda i: (i, 0))] * 2
        ),
        name="product",
    )(matrix, probes)

    skeletons = leaf_skeleton
    for bit in range(leaf_bits):
        partner = lax.ppermute(skeletons, "leaf", [(p, p ^ 1 << bit) for p in range(n_leaf)])
        if bit == 0:
            send, partner = lax.optimization_barrier((send, partner))
        skeletons = jnp.where(
            leaf_pos >> bit & 1 == 1,
            jnp.concatenate([partner, skeletons], axis=0),
            jnp.concatenate([skeletons, partner], axis=0),
        )
    top_received = across(send)
    tables = skeletons[:, None, :]

    def ordered(group):
        high, count = group[0], len(group)
        outs = pl.pallas_call(
            lambda *refs: ordered_kernel(n_leaf, n_grp, high, *refs),
            out_shape=(slim,) * (4 * count),
            grid_spec=grid_spec(
                2 * count,
                [*matrix_specs(high), picked_spec(high)],
                [pl.BlockSpec(slim.shape, lambda i: (0, 0))] * (4 * count),
            ),
            name="ordered",
        )
        outs = outs(matrix, probes, tables)
        return {mask: outs[4 * j : 4 * j + 4] for j, mask in enumerate(group)}

    pieces = {}
    for at in range(1, spots, GROUP):
        pieces.update(ordered(masks[at : at + GROUP]))

    piece = pl.BlockSpec((leaf_rows, half), lambda i: (i, 0))
    part = pl.BlockSpec((rank, half), lambda i: (i, 0))
    first, second = {}, {}
    split = pl.pallas_call(
        split_kernel,
        out_shape=(slim,) * 2,
        grid_spec=grid_spec(2, [piece, piece, picked_spec(top)], [part] * 2),
        name="split",
    )
    first[top], second[top] = split(keep, top_received, tables)

    for mask in masks[1:]:
        received = across(pieces[mask][0])
        first[mask] = pieces[mask][1] + received
        if mask == min(1, top):
            gate = received
    for mask in masks[1:]:
        send, _ = lax.optimization_barrier((pieces[mask][2], gate))
        second[mask] = pieces[mask][3] + across(send)

    def gathered(values, gates=None):
        values = dict(values)
        for mask in masks[:-1]:
            bit = mask & -mask
            value = values[mask]
            if gates is not None:
                gate = gates[0] if mask == top else gates[1]
                value, _ = lax.optimization_barrier((value, gate))
            elif mask ^ bit == 0:
                early.append(value)
            arrived = along(
                value, [(z, z ^ bit) for z in range(spots)]
            )
            if gates is not None and mask != top:
                arrived, _ = lax.optimization_barrier((arrived, gates[2]))
            values[mask ^ bit] = values[mask ^ bit] + arrived
        return values[0]

    early = []

    skeleton_rows = gathered(first)

    def cross_of(stacked, rows):
        return dot(stacked, rows, ((1,), (1,)))

    halves = (skeleton_rows[:rank], skeleton_rows[rank:])
    grams = [cross_of(r, r) for r in halves]
    own_gram = jnp.where(side == 0, grams[0], grams[1])
    received_gram = across(jnp.where(side == 0, grams[1], grams[0]))

    def level_offset(level):
        return sum(all_leaves >> inner for inner in range(1, level))

    def picked_of(level):
        node = level_offset(level) + (device >> level)
        return lax.dynamic_slice_in_dim(node_skeleton, node, 1, 0)[0]

    gates = []

    def taken(stacked, picked):
        index = jnp.arange(stacked.shape[0], dtype=jnp.int32)
        return dot((picked[:, None] == index[None, :]).astype(jnp.float32), stacked)

    low_stack = skeleton_rows
    low_picked = picked_of(1)
    node_own = device >> 1
    current = taken(low_stack, low_picked)
    low_cross = high_cross = cross_of(low_stack, current)
    even = device - side
    for level in range(2, levels + 1):
        if level <= leaf_bits:
            bit = level - 2
            hops = [(z, z ^ 1 << bit) for z in range(0, spots, 1 << bit)]
            partner = along(current, hops)
            upper = spot >> bit & 1
            gates.append(partner)
        else:
            bit = level - leaf_bits - 1
            pairs = [
                (g * n_leaf + s, (g ^ 1 << bit) * n_leaf + s)
                for g in range(0, n_grp, 1 << bit)
                for s in range(2)
            ]
            send = lambda value: lax.ppermute(value, ("grp", "leaf"), pairs)
            partner = send(current)
            upper = grp_pos >> bit & 1
        stacked = jnp.concatenate(
            [
                jnp.where(upper == 1, partner, current),
                jnp.where(upper == 1, current, partner),
            ],
            axis=0,
        )
        picked = picked_of(level)
        current = taken(stacked, picked)
        select = even % (1 << level) == 1 << level - 1
        if level == levels:
            select = select | (even == 0)
        high_cross = jnp.where(select, cross_of(stacked, current), high_cross)
        node = level_offset(level) + (device >> level)
        node_own = jnp.where(select & (side == 0), node, node_own)

    other_rows = gathered(second, [early[0], gates[0], current])
    crosses = [
        cross_of(z, r) for z, r in zip((other_rows[:rank], other_rows[rank:]), halves)
    ]
    own = jnp.concatenate(
        [
            jnp.where(side == 0, crosses[0], crosses[1]),
            jnp.where(side == 1, low_cross, high_cross),
        ],
        axis=0,
    )
    sent = jnp.concatenate(
        [
            jnp.where(side == 0, crosses[1], crosses[0]),
            jnp.where(side == 1, high_cross, low_cross),
        ],
        axis=0,
    )
    received = across(sent)
    square = jax.ShapeDtypeStruct((rank, rank), jnp.float32)
    inverse = pl.pallas_call(inverse_kernel, out_shape=square, name="inverse")(own_gram, received_gram)
    tall = [jax.ShapeDtypeStruct((rows, rank), jnp.float32) for rows in (leaf_rows, 2 * rank)]
    whole = pl.BlockSpec(memory_space=pltpu.VMEM)
    leaf_basis, transfer = pl.pallas_call(
        finish_kernel,
        out_shape=tall,
        in_specs=[pl.BlockSpec(memory_space=pltpu.SMEM)] + [whole] * 5,
        name="finish",
    )(node_own[None], own, received, inverse, leaf_skeleton, node_skeleton)
    return (leaf_basis, transfer[None])


def solution(mesh):
    return jax.shard_map(
        on_device,
        mesh=mesh,
        in_specs=(P("grp", "leaf"), P("leaf", None), P(("grp", "leaf"), None), P()),
        out_specs=(P(("grp", "leaf"), None), P(("grp", "leaf"), None, None)),
        check_vma=False,
    )
```

```python
import jax
import jax.numpy as jnp
from jax import lax
from jax.experimental import pallas as pl
from jax.experimental.pallas import tpu as pltpu
from jax.sharding import PartitionSpec as P


HIGHEST = lax.Precision.HIGHEST
GROUP = 1


def bits_of(count):
    return count.bit_length() - 1


def spd_inverse(a):
    n = a.shape[0]
    tiles = [a[8 * r : 8 * r + 8, :] for r in range(n // 8)]
    lane = lax.broadcasted_iota(jnp.int32, (8, n), 1)
    sub = lax.broadcasted_iota(jnp.int32, (8, n), 0)
    for kb in range(n // 8):
        k = 8 * kb
        edge = [jnp.broadcast_to(tiles[kb][:, k + j : k + j + 1], (8, n)) for j in range(8)]
        d = {
            (i, j): jnp.broadcast_to(edge[j][i : i + 1, :], (8, n))
            for i in range(8)
            for j in range(i + 1)
        }
        inside = (lane >= k) & (lane < k + 8)
        base = jnp.where(inside, jnp.where(lane - k == sub, 1.0, 0.0), tiles[kb])
        p = [jnp.broadcast_to(base[j : j + 1, :], (8, n)) for j in range(8)]
        inv, low = [None] * 8, {}
        for j in range(8):
            inv[j] = 1.0 / d[j, j]
            for i in range(j + 1, 8):
                low[i, j] = d[i, j] * inv[j]
            for i in range(j + 1, 8):
                for m in range(j + 1, i + 1):
                    d[i, m] = d[i, m] - low[i, j] * d[m, j]
                p[i] = p[i] - low[i, j] * p[j]
        w = [p[j] * inv[j] for j in range(8)]
        for j in range(7, 0, -1):
            for i in range(j):
                w[i] = w[i] - low[j, i] * w[j]
        fresh = []
        for r, t in enumerate(tiles):
            if r == kb:
                x = w[0]
                for j in range(1, 8):
                    x = jnp.where(sub == j, w[j], x)
            else:
                x = jnp.where(inside, 0.0, t)
                col = [jnp.broadcast_to(t[:, k + j : k + j + 1], (8, n)) for j in range(8)]
                pairs = [col[j] * w[j] + col[j + 1] * w[j + 1] for j in range(0, 8, 2)]
                x = x - ((pairs[0] + pairs[1]) + (pairs[2] + pairs[3]))
            fresh.append(x)
        tiles = fresh
    return jnp.concatenate(tiles, axis=0)


def dot(a, b, dims=((1,), (0,)), precision=HIGHEST):
    return lax.dot_general(
        a, b, (dims, ((), ())), precision=precision, preferred_element_type=jnp.float32
    )


def choices(picked, count):
    rank = picked.shape[1]
    index = lax.broadcasted_iota(jnp.int32, (count, rank), 0)
    chosen = index == picked
    ahead = jnp.sum((picked < index).astype(jnp.float32), axis=1, keepdims=True)
    member = jnp.sum(chosen.astype(jnp.float32), axis=1, keepdims=True)
    place = index.astype(jnp.float32) - ahead
    slot = lax.broadcasted_iota(jnp.int32, (count, rank), 1).astype(jnp.float32)
    others = (slot == place) & (jnp.broadcast_to(member, place.shape) < 0.5)
    return chosen.astype(jnp.float32), others.astype(jnp.float32)


def inverse_kernel(gram_ref, out_ref):
    out_ref[...] = spd_inverse(gram_ref[...])


def finish_kernel(
    node_at, total_ref, inverse_ref, picked_ref, table_ref, leaf_ref, node_ref
):
    rank = total_ref.shape[1]
    cross = total_ref[rank:, :]
    index = lax.broadcasted_iota(jnp.int32, cross.shape, 0)
    choice = (index == table_ref[pl.ds(node_at[0], 1), :]).astype(jnp.float32)
    gram = dot(choice, cross, ((0,), (0,)))
    chosen, others = choices(picked_ref[...], leaf_ref.shape[0])
    leaf_ref[...] = chosen + dot(others, dot(total_ref[:rank, :], inverse_ref[...]))
    node_ref[...] = dot(cross, spd_inverse(gram))


def unit_rows(matrix_ref, hit, n_grp):
    rows = matrix_ref.shape[0]
    pieces = []
    for c in range(n_grp):
        piece = matrix_ref[:, c * rows : (c + 1) * rows]
        pieces.append(jnp.where(hit == c, jnp.zeros_like(piece), piece))
    return pieces


def sides(block, probes_ref, side, half):
    away = probes_ref[:, pl.ds(pl.multiple_of((1 - side) * half, half), half)]
    home = probes_ref[:, pl.ds(pl.multiple_of(side * half, half), half)]
    return dot(block, away, precision=None), dot(block, home, precision=None)


def plain_kernel(n_leaf, n_grp, mask, matrix_ref, probes_ref, send_ref, keep_ref):
    spot = (lax.axis_index("leaf") >> 1) ^ mask
    hit = lax.axis_index("grp") * n_leaf + 2 * spot + pl.program_id(0) - lax.axis_index("leaf") * n_grp
    block = jnp.concatenate(unit_rows(matrix_ref, hit, n_grp), axis=1)
    send_ref[...], keep_ref[...] = sides(block, probes_ref, lax.axis_index("leaf") & 1, send_ref.shape[1])


def ordered_kernel(n_leaf, n_grp, high, matrix_ref, probes_ref, picked_ref, *outs):
    step = pl.program_id(0)
    spot = (lax.axis_index("leaf") >> 1) ^ (high - step // 2)
    hit = lax.axis_index("grp") * n_leaf + 2 * spot + step % 2 - lax.axis_index("leaf") * n_grp
    rank, half = picked_ref.shape[2], outs[0].shape[1]
    chosen, others = choices(picked_ref[0], matrix_ref.shape[0])
    order = jnp.concatenate([chosen, others], axis=1).astype(jnp.bfloat16)
    block = jnp.concatenate(
        [
            dot(order, piece, ((0,), (0,)), None).astype(jnp.bfloat16)
            for piece in unit_rows(matrix_ref, hit, n_grp)
        ],
        axis=1,
    )
    away, home = sides(block, probes_ref, lax.axis_index("leaf") & 1, half)
    for j in range(len(outs) // 4):

        @pl.when(step // 2 == j)
        def _():
            at = pl.ds(pl.multiple_of(step % 2 * rank, rank), rank)
            outs[4 * j][at, :] = away[:rank]
            outs[4 * j + 1][at, :] = home[:rank]
            outs[4 * j + 2][at, :] = away[rank:]
            outs[4 * j + 3][at, :] = home[rank:]


def split_kernel(keep_ref, received_ref, picked_ref, first_ref, second_ref):
    total = keep_ref[...] + received_ref[...]
    order = jnp.concatenate(choices(picked_ref[0], total.shape[0]), axis=1).astype(jnp.bfloat16)
    moved = None
    for _ in range(3):
        part = total.astype(jnp.bfloat16)
        total = total - part.astype(jnp.float32)
        value = dot(order, part, ((0,), (0,)), None)
        moved = value if moved is None else moved + value
    rank = first_ref.shape[0]
    first_ref[...] = moved[:rank]
    second_ref[...] = moved[rank:]


def on_device(matrix, probes, leaf_skeleton, node_skeleton):
    n_grp = lax.axis_size("grp")
    n_leaf = lax.axis_size("leaf")
    grp_pos = lax.axis_index("grp")
    leaf_pos = lax.axis_index("leaf")
    device = grp_pos * n_leaf + leaf_pos
    side = leaf_pos & 1
    spot = leaf_pos >> 1
    spots = n_leaf // 2
    row_count, col_count = matrix.shape
    leaf_rows = row_count // n_leaf
    half = probes.shape[1] // 2
    rank = leaf_skeleton.shape[1]
    all_leaves = n_grp * n_leaf
    leaf_bits, grp_bits = bits_of(n_leaf), bits_of(n_grp)
    levels = leaf_bits + grp_bits

    def across(value):
        return lax.ppermute(value, "leaf", [(p, p ^ 1) for p in range(n_leaf)])

    def along(value, hops):
        pairs = [(2 * a + s, 2 * b + s) for a, b in hops for s in range(2)]
        return lax.ppermute(value, "leaf", pairs)

    masks = list(range(spots - 1, -1, -1))
    top = masks[0]
    wide = jax.ShapeDtypeStruct((2 * leaf_rows, half), jnp.float32)
    slim = jax.ShapeDtypeStruct((2 * rank, half), jnp.float32)

    def leaf_row(high):
        return lambda i: 2 * ((lax.axis_index("leaf") >> 1) ^ (high - i // 2)) + i % 2

    def grid_spec(count, in_specs, out_specs):
        return pl.GridSpec(grid=(count,), in_specs=in_specs, out_specs=out_specs)

    def matrix_specs(high):
        row = leaf_row(high)
        return [
            pl.BlockSpec((leaf_rows, col_count), lambda i: (row(i), 0)),
            pl.BlockSpec(memory_space=pltpu.VMEM),
        ]

    def picked_spec(high):
        row = leaf_row(high)
        return pl.BlockSpec((1, 1, rank), lambda i: (row(i), 0, 0))

    send, keep = pl.pallas_call(
        lambda *refs: plain_kernel(n_leaf, n_grp, top, *refs),
        out_shape=(wide,) * 2,
        grid_spec=grid_spec(
            2, matrix_specs(top), [pl.BlockSpec((leaf_rows, half), lambda i: (i, 0))] * 2
        ),
        name="product",
    )(matrix, probes)

    skeletons = leaf_skeleton
    for bit in range(leaf_bits):
        partner = lax.ppermute(skeletons, "leaf", [(p, p ^ 1 << bit) for p in range(n_leaf)])
        if bit == 0:
            send, partner = lax.optimization_barrier((send, partner))
        skeletons = jnp.where(
            leaf_pos >> bit & 1 == 1,
            jnp.concatenate([partner, skeletons], axis=0),
            jnp.concatenate([skeletons, partner], axis=0),
        )
    top_received = across(send)
    tables = skeletons[:, None, :]

    def ordered(group):
        high, count = group[0], len(group)
        outs = pl.pallas_call(
            lambda *refs: ordered_kernel(n_leaf, n_grp, high, *refs),
            out_shape=(slim,) * (4 * count),
            grid_spec=grid_spec(
                2 * count,
                [*matrix_specs(high), picked_spec(high)],
                [pl.BlockSpec(slim.shape, lambda i: (0, 0))] * (4 * count),
            ),
            name="ordered",
        )
        outs = outs(matrix, probes, tables)
        return {mask: outs[4 * j : 4 * j + 4] for j, mask in enumerate(group)}

    pieces = {}
    for at in range(1, spots, GROUP):
        pieces.update(ordered(masks[at : at + GROUP]))

    piece = pl.BlockSpec((leaf_rows, half), lambda i: (i, 0))
    part = pl.BlockSpec((rank, half), lambda i: (i, 0))
    first, second = {}, {}
    split = pl.pallas_call(
        split_kernel,
        out_shape=(slim,) * 2,
        grid_spec=grid_spec(2, [piece, piece, picked_spec(top)], [part] * 2),
        name="split",
    )
    first[top], second[top] = split(keep, top_received, tables)

    for mask in masks[1:]:
        received = across(pieces[mask][0])
        first[mask] = pieces[mask][1] + received
        if mask == min(1, top):
            gate = received
    for mask in masks[1:]:
        send, _ = lax.optimization_barrier((pieces[mask][2], gate))
        second[mask] = pieces[mask][3] + across(send)

    def gathered(values, gates=None):
        values = dict(values)
        for mask in masks[:-1]:
            bit = mask & -mask
            value = values[mask]
            if gates is not None:
                gate = gates[0] if mask == top else gates[1]
                value, _ = lax.optimization_barrier((value, gate))
            elif mask ^ bit == 0:
                early.append(value)
            arrived = along(
                value, [(z, z ^ bit) for z in range(spots)]
            )
            if gates is not None and mask != top:
                arrived, _ = lax.optimization_barrier((arrived, gates[2]))
            values[mask ^ bit] = values[mask ^ bit] + arrived
        return values[0]

    early = []

    skeleton_rows = gathered(first)

    def cross_of(stacked, rows):
        return dot(stacked, rows, ((1,), (1,)))

    halves = (skeleton_rows[:rank], skeleton_rows[rank:])
    grams = [cross_of(r, r) for r in halves]
    own_gram = jnp.where(side == 0, grams[0], grams[1])
    received_gram = across(jnp.where(side == 0, grams[1], grams[0]))

    def level_offset(level):
        return sum(all_leaves >> inner for inner in range(1, level))

    def picked_of(level):
        node = level_offset(level) + (device >> level)
        return lax.dynamic_slice_in_dim(node_skeleton, node, 1, 0)[0]

    gates = []

    def taken(stacked, picked):
        index = jnp.arange(stacked.shape[0], dtype=jnp.int32)
        return dot((picked[:, None] == index[None, :]).astype(jnp.float32), stacked)

    low_stack = skeleton_rows
    low_picked = picked_of(1)
    node_own = device >> 1
    current = taken(low_stack, low_picked)
    low_cross = high_cross = cross_of(low_stack, current)
    even = device - side
    for level in range(2, levels + 1):
        if level <= leaf_bits:
            bit = level - 2
            hops = [(z, z ^ 1 << bit) for z in range(0, spots, 1 << bit)]
            partner = along(current, hops)
            upper = spot >> bit & 1
            gates.append(partner)
        else:
            bit = level - leaf_bits - 1
            pairs = [
                (g * n_leaf + s, (g ^ 1 << bit) * n_leaf + s)
                for g in range(0, n_grp, 1 << bit)
                for s in range(2)
            ]
            send = lambda value: lax.ppermute(value, ("grp", "leaf"), pairs)
            partner = send(current)
            upper = grp_pos >> bit & 1
        before = current
        if level == levels:
            partner, gram = lax.optimization_barrier((partner, own_gram + received_gram))
        stacked = jnp.concatenate(
            [
                jnp.where(upper == 1, partner, current),
                jnp.where(upper == 1, current, partner),
            ],
            axis=0,
        )
        picked = picked_of(level)
        current = taken(stacked, picked)
        select = even % (1 << level) == 1 << level - 1
        if level == levels:
            select = select | (even == 0)
        high_cross = jnp.where(select, cross_of(stacked, current), high_cross)
        node = level_offset(level) + (device >> level)
        node_own = jnp.where(select & (side == 0), node, node_own)

    other_rows = gathered(second, [early[0], gates[0], before])
    crosses = [
        cross_of(z, r) for z, r in zip((other_rows[:rank], other_rows[rank:]), halves)
    ]
    sent = jnp.concatenate(
        [
            jnp.where(side == 0, crosses[1], crosses[0]),
            jnp.where(side == 1, high_cross, low_cross),
        ],
        axis=0,
    )
    received = across(sent)
    own = jnp.concatenate(
        [
            jnp.where(side == 0, crosses[0], crosses[1]),
            jnp.where(side == 1, low_cross, high_cross),
        ],
        axis=0,
    )
    total = own + received
    square = jax.ShapeDtypeStruct((rank, rank), jnp.float32)
    inverse = pl.pallas_call(inverse_kernel, out_shape=square, name="inverse")(gram)
    tall = [jax.ShapeDtypeStruct((rows, rank), jnp.float32) for rows in (leaf_rows, 2 * rank)]
    whole = pl.BlockSpec(memory_space=pltpu.VMEM)
    leaf_basis, transfer = pl.pallas_call(
        finish_kernel,
        out_shape=tall,
        in_specs=[pl.BlockSpec(memory_space=pltpu.SMEM)] + [whole] * 4,
        name="finish",
    )(
        node_own[None], total, inverse, leaf_skeleton, node_skeleton
    )
    return (leaf_basis, transfer[None])


def solution(mesh):
    return jax.shard_map(
        on_device,
        mesh=mesh,
        in_specs=(P("grp", "leaf"), P("leaf", None), P(("grp", "leaf"), None), P()),
        out_specs=(P(("grp", "leaf"), None), P(("grp", "leaf"), None, None)),
        check_vma=False,
    )
```

```python
import jax
import jax.numpy as jnp
from jax import lax
from jax.experimental import pallas as pl
from jax.experimental.pallas import tpu as pltpu
from jax.sharding import PartitionSpec as P


HIGHEST = lax.Precision.HIGHEST
GROUP = 1


def bits_of(count):
    return count.bit_length() - 1


def spd_inverse(a):
    n = a.shape[0]
    tiles = [a[8 * r : 8 * r + 8, :] for r in range(n // 8)]
    lane = lax.broadcasted_iota(jnp.int32, (8, n), 1)
    sub = lax.broadcasted_iota(jnp.int32, (8, n), 0)
    for kb in range(n // 8):
        k = 8 * kb
        edge = [jnp.broadcast_to(tiles[kb][:, k + j : k + j + 1], (8, n)) for j in range(8)]
        inside = (lane >= k) & (lane < k + 8)
        w = jnp.where(inside, jnp.where(lane - k == sub, 1.0, 0.0), tiles[kb])
        for j in range(8):
            pivot = 1.0 / jnp.broadcast_to(edge[j][j : j + 1, :], (8, n))
            mine = sub == j
            factor = jnp.where(mine, 0.0, edge[j])
            scaled = jnp.broadcast_to(w[j : j + 1, :], (8, n)) * pivot
            w = jnp.where(mine, scaled, w - factor * scaled)
            for i in range(j + 1, 8):
                scaled = jnp.broadcast_to(edge[i][j : j + 1, :], (8, n)) * pivot
                edge[i] = jnp.where(mine, scaled, edge[i] - factor * scaled)
        solved = w
        w = [jnp.broadcast_to(solved[j : j + 1, :], (8, n)) for j in range(8)]
        fresh = []
        for r, t in enumerate(tiles):
            if r == kb:
                x = solved
            else:
                x = jnp.where(inside, 0.0, t)
                col = [jnp.broadcast_to(t[:, k + j : k + j + 1], (8, n)) for j in range(8)]
                pairs = [col[j] * w[j] + col[j + 1] * w[j + 1] for j in range(0, 8, 2)]
                x = x - ((pairs[0] + pairs[1]) + (pairs[2] + pairs[3]))
            fresh.append(x)
        tiles = fresh
    return jnp.concatenate(tiles, axis=0)


def dot(a, b, dims=((1,), (0,)), precision=HIGHEST):
    return lax.dot_general(
        a, b, (dims, ((), ())), precision=precision, preferred_element_type=jnp.float32
    )


def choices(picked, count):
    rank = picked.shape[1]
    index = lax.broadcasted_iota(jnp.int32, (count, rank), 0)
    chosen = index == picked
    ahead = jnp.sum((picked < index).astype(jnp.float32), axis=1, keepdims=True)
    member = jnp.sum(chosen.astype(jnp.float32), axis=1, keepdims=True)
    place = index.astype(jnp.float32) - ahead
    slot = lax.broadcasted_iota(jnp.int32, (count, rank), 1).astype(jnp.float32)
    others = (slot == place) & (jnp.broadcast_to(member, place.shape) < 0.5)
    return chosen.astype(jnp.float32), others.astype(jnp.float32)


def inverse_kernel(gram_ref, out_ref):
    out_ref[...] = spd_inverse(gram_ref[...])


def finish_kernel(
    node_at, total_ref, inverse_ref, picked_ref, table_ref, leaf_ref, node_ref
):
    rank = total_ref.shape[1]
    cross = total_ref[rank:, :]
    index = lax.broadcasted_iota(jnp.int32, cross.shape, 0)
    choice = (index == table_ref[pl.ds(node_at[0], 1), :]).astype(jnp.float32)
    gram = dot(choice, cross, ((0,), (0,)))
    chosen, others = choices(picked_ref[...], leaf_ref.shape[0])
    leaf_ref[...] = chosen + dot(others, dot(total_ref[:rank, :], inverse_ref[...]))
    node_ref[...] = dot(cross, spd_inverse(gram))


def unit_rows(matrix_ref, hit, n_grp):
    rows = matrix_ref.shape[0]
    pieces = []
    for c in range(n_grp):
        piece = matrix_ref[:, c * rows : (c + 1) * rows]
        pieces.append(jnp.where(hit == c, jnp.zeros_like(piece), piece))
    return pieces


def sides(block, probes_ref, side, half):
    away = probes_ref[:, pl.ds(pl.multiple_of((1 - side) * half, half), half)]
    home = probes_ref[:, pl.ds(pl.multiple_of(side * half, half), half)]
    return dot(block, away, precision=None), dot(block, home, precision=None)


def plain_kernel(n_leaf, n_grp, mask, matrix_ref, probes_ref, send_ref, keep_ref):
    spot = (lax.axis_index("leaf") >> 1) ^ mask
    hit = lax.axis_index("grp") * n_leaf + 2 * spot + pl.program_id(0) - lax.axis_index("leaf") * n_grp
    block = jnp.concatenate(unit_rows(matrix_ref, hit, n_grp), axis=1)
    send_ref[...], keep_ref[...] = sides(block, probes_ref, lax.axis_index("leaf") & 1, send_ref.shape[1])


def ordered_kernel(n_leaf, n_grp, high, matrix_ref, probes_ref, picked_ref, *outs):
    step = pl.program_id(0)
    spot = (lax.axis_index("leaf") >> 1) ^ (high - step // 2)
    hit = lax.axis_index("grp") * n_leaf + 2 * spot + step % 2 - lax.axis_index("leaf") * n_grp
    rank, half = picked_ref.shape[2], outs[0].shape[1]
    chosen, others = choices(picked_ref[0], matrix_ref.shape[0])
    order = jnp.concatenate([chosen, others], axis=1).astype(jnp.bfloat16)
    block = jnp.concatenate(
        [
            dot(order, piece, ((0,), (0,)), None).astype(jnp.bfloat16)
            for piece in unit_rows(matrix_ref, hit, n_grp)
        ],
        axis=1,
    )
    away, home = sides(block, probes_ref, lax.axis_index("leaf") & 1, half)
    for j in range(len(outs) // 4):

        @pl.when(step // 2 == j)
        def _():
            at = pl.ds(pl.multiple_of(step % 2 * rank, rank), rank)
            outs[4 * j][at, :] = away[:rank]
            outs[4 * j + 1][at, :] = home[:rank]
            outs[4 * j + 2][at, :] = away[rank:]
            outs[4 * j + 3][at, :] = home[rank:]


def split_kernel(keep_ref, received_ref, picked_ref, first_ref, second_ref):
    total = keep_ref[...] + received_ref[...]
    order = jnp.concatenate(choices(picked_ref[0], total.shape[0]), axis=1).astype(jnp.bfloat16)
    moved = None
    for _ in range(3):
        part = total.astype(jnp.bfloat16)
        total = total - part.astype(jnp.float32)
        value = dot(order, part, ((0,), (0,)), None)
        moved = value if moved is None else moved + value
    rank = first_ref.shape[0]
    first_ref[...] = moved[:rank]
    second_ref[...] = moved[rank:]


def on_device(matrix, probes, leaf_skeleton, node_skeleton):
    n_grp = lax.axis_size("grp")
    n_leaf = lax.axis_size("leaf")
    grp_pos = lax.axis_index("grp")
    leaf_pos = lax.axis_index("leaf")
    device = grp_pos * n_leaf + leaf_pos
    side = leaf_pos & 1
    spot = leaf_pos >> 1
    spots = n_leaf // 2
    row_count, col_count = matrix.shape
    leaf_rows = row_count // n_leaf
    half = probes.shape[1] // 2
    rank = leaf_skeleton.shape[1]
    all_leaves = n_grp * n_leaf
    leaf_bits, grp_bits = bits_of(n_leaf), bits_of(n_grp)
    levels = leaf_bits + grp_bits

    def across(value):
        return lax.ppermute(value, "leaf", [(p, p ^ 1) for p in range(n_leaf)])

    def along(value, hops):
        pairs = [(2 * a + s, 2 * b + s) for a, b in hops for s in range(2)]
        return lax.ppermute(value, "leaf", pairs)

    masks = list(range(spots - 1, -1, -1))
    top = masks[0]
    wide = jax.ShapeDtypeStruct((2 * leaf_rows, half), jnp.float32)
    slim = jax.ShapeDtypeStruct((2 * rank, half), jnp.float32)

    def leaf_row(high):
        return lambda i: 2 * ((lax.axis_index("leaf") >> 1) ^ (high - i // 2)) + i % 2

    def grid_spec(count, in_specs, out_specs):
        return pl.GridSpec(grid=(count,), in_specs=in_specs, out_specs=out_specs)

    def matrix_specs(high):
        row = leaf_row(high)
        return [
            pl.BlockSpec((leaf_rows, col_count), lambda i: (row(i), 0)),
            pl.BlockSpec(memory_space=pltpu.VMEM),
        ]

    def picked_spec(high):
        row = leaf_row(high)
        return pl.BlockSpec((1, 1, rank), lambda i: (row(i), 0, 0))

    send, keep = pl.pallas_call(
        lambda *refs: plain_kernel(n_leaf, n_grp, top, *refs),
        out_shape=(wide,) * 2,
        grid_spec=grid_spec(
            2, matrix_specs(top), [pl.BlockSpec((leaf_rows, half), lambda i: (i, 0))] * 2
        ),
        name="product",
    )(matrix, probes)

    skeletons = leaf_skeleton
    for bit in range(leaf_bits):
        partner = lax.ppermute(skeletons, "leaf", [(p, p ^ 1 << bit) for p in range(n_leaf)])
        if bit == 0:
            send, partner = lax.optimization_barrier((send, partner))
        skeletons = jnp.where(
            leaf_pos >> bit & 1 == 1,
            jnp.concatenate([partner, skeletons], axis=0),
            jnp.concatenate([skeletons, partner], axis=0),
        )
    top_received = across(send)
    tables = skeletons[:, None, :]

    def ordered(group):
        high, count = group[0], len(group)
        outs = pl.pallas_call(
            lambda *refs: ordered_kernel(n_leaf, n_grp, high, *refs),
            out_shape=(slim,) * (4 * count),
            grid_spec=grid_spec(
                2 * count,
                [*matrix_specs(high), picked_spec(high)],
                [pl.BlockSpec(slim.shape, lambda i: (0, 0))] * (4 * count),
            ),
            name="ordered",
        )
        outs = outs(matrix, probes, tables)
        return {mask: outs[4 * j : 4 * j + 4] for j, mask in enumerate(group)}

    pieces = {}
    for at in range(1, spots, GROUP):
        pieces.update(ordered(masks[at : at + GROUP]))

    piece = pl.BlockSpec((leaf_rows, half), lambda i: (i, 0))
    part = pl.BlockSpec((rank, half), lambda i: (i, 0))
    first, second = {}, {}
    split = pl.pallas_call(
        split_kernel,
        out_shape=(slim,) * 2,
        grid_spec=grid_spec(2, [piece, piece, picked_spec(top)], [part] * 2),
        name="split",
    )
    first[top], second[top] = split(keep, top_received, tables)

    for mask in masks[1:]:
        received = across(pieces[mask][0])
        first[mask] = pieces[mask][1] + received
        if mask == min(1, top):
            gate = received
    for mask in masks[1:]:
        send, _ = lax.optimization_barrier((pieces[mask][2], gate))
        second[mask] = pieces[mask][3] + across(send)

    def gathered(values, gates=None):
        values = dict(values)
        for mask in masks[:-1]:
            bit = mask & -mask
            value = values[mask]
            if gates is not None:
                gate = gates[0] if mask == top else gates[1]
                value, _ = lax.optimization_barrier((value, gate))
            elif mask ^ bit == 0:
                early.append(value)
            arrived = along(
                value, [(z, z ^ bit) for z in range(spots)]
            )
            if gates is not None and mask != top:
                arrived, _ = lax.optimization_barrier((arrived, gates[2]))
            values[mask ^ bit] = values[mask ^ bit] + arrived
        return values[0]

    early = []

    skeleton_rows = gathered(first)

    def cross_of(stacked, rows):
        return dot(stacked, rows, ((1,), (1,)))

    halves = (skeleton_rows[:rank], skeleton_rows[rank:])
    grams = [cross_of(r, r) for r in halves]
    own_gram = jnp.where(side == 0, grams[0], grams[1])
    received_gram = across(jnp.where(side == 0, grams[1], grams[0]))

    def level_offset(level):
        return sum(all_leaves >> inner for inner in range(1, level))

    def picked_of(level):
        node = level_offset(level) + (device >> level)
        return lax.dynamic_slice_in_dim(node_skeleton, node, 1, 0)[0]

    gates = []

    def taken(stacked, picked):
        index = jnp.arange(stacked.shape[0], dtype=jnp.int32)
        return dot((picked[:, None] == index[None, :]).astype(jnp.float32), stacked)

    low_stack = skeleton_rows
    low_picked = picked_of(1)
    node_own = device >> 1
    current = taken(low_stack, low_picked)
    low_cross = high_cross = cross_of(low_stack, current)
    even = device - side
    for level in range(2, levels + 1):
        if level <= leaf_bits:
            bit = level - 2
            hops = [(z, z ^ 1 << bit) for z in range(0, spots, 1 << bit)]
            partner = along(current, hops)
            upper = spot >> bit & 1
            gates.append(partner)
        else:
            bit = level - leaf_bits - 1
            pairs = [
                (g * n_leaf + s, (g ^ 1 << bit) * n_leaf + s)
                for g in range(0, n_grp, 1 << bit)
                for s in range(2)
            ]
            send = lambda value: lax.ppermute(value, ("grp", "leaf"), pairs)
            partner = send(current)
            upper = grp_pos >> bit & 1
        before = current
        if level == levels:
            partner, gram = lax.optimization_barrier((partner, own_gram + received_gram))
        stacked = jnp.concatenate(
            [
                jnp.where(upper == 1, partner, current),
                jnp.where(upper == 1, current, partner),
            ],
            axis=0,
        )
        picked = picked_of(level)
        current = taken(stacked, picked)
        select = even % (1 << level) == 1 << level - 1
        if level == levels:
            select = select | (even == 0)
        high_cross = jnp.where(select, cross_of(stacked, current), high_cross)
        node = level_offset(level) + (device >> level)
        node_own = jnp.where(select & (side == 0), node, node_own)

    other_rows = gathered(second, [early[0], gates[0], before])
    crosses = [
        cross_of(z, r) for z, r in zip((other_rows[:rank], other_rows[rank:]), halves)
    ]
    sent = jnp.concatenate(
        [
            jnp.where(side == 0, crosses[1], crosses[0]),
            jnp.where(side == 1, high_cross, low_cross),
        ],
        axis=0,
    )
    received = across(sent)
    own = jnp.concatenate(
        [
            jnp.where(side == 0, crosses[0], crosses[1]),
            jnp.where(side == 1, low_cross, high_cross),
        ],
        axis=0,
    )
    total = own + received
    square = jax.ShapeDtypeStruct((rank, rank), jnp.float32)
    inverse = pl.pallas_call(inverse_kernel, out_shape=square, name="inverse")(gram)
    tall = [jax.ShapeDtypeStruct((rows, rank), jnp.float32) for rows in (leaf_rows, 2 * rank)]
    whole = pl.BlockSpec(memory_space=pltpu.VMEM)
    leaf_basis, transfer = pl.pallas_call(
        finish_kernel,
        out_shape=tall,
        in_specs=[pl.BlockSpec(memory_space=pltpu.SMEM)] + [whole] * 4,
        name="finish",
    )(
        node_own[None], total, inverse, leaf_skeleton, node_skeleton
    )
    return (leaf_basis, transfer[None])


def solution(mesh):
    return jax.shard_map(
        on_device,
        mesh=mesh,
        in_specs=(P("grp", "leaf"), P("leaf", None), P(("grp", "leaf"), None), P()),
        out_specs=(P(("grp", "leaf"), None), P(("grp", "leaf"), None, None)),
        check_vma=False,
    )
```

```python
import jax
import jax.numpy as jnp
from jax import lax
from jax.experimental import pallas as pl
from jax.experimental.pallas import tpu as pltpu
from jax.sharding import PartitionSpec as P


HIGHEST = lax.Precision.HIGHEST
GROUP = 1


def bits_of(count):
    return count.bit_length() - 1


def spd_inverse(a):
    n = a.shape[0]
    tiles = [a[8 * r : 8 * r + 8, :] for r in range(n // 8)]
    lane = lax.broadcasted_iota(jnp.int32, (8, n), 1)
    sub = lax.broadcasted_iota(jnp.int32, (8, n), 0)
    for kb in range(n // 8):
        k = 8 * kb
        edge = [jnp.broadcast_to(tiles[kb][:, k + j : k + j + 1], (8, n)) for j in range(8)]
        inside = (lane >= k) & (lane < k + 8)
        w = jnp.where(inside, jnp.where(lane - k == sub, 1.0, 0.0), tiles[kb])
        for j in range(8):
            pivot = 1.0 / jnp.broadcast_to(edge[j][j : j + 1, :], (8, n))
            mine = sub == j
            factor = jnp.where(mine, 0.0, edge[j])
            scaled = jnp.broadcast_to(w[j : j + 1, :], (8, n)) * pivot
            w = jnp.where(mine, scaled, w - factor * scaled)
            for i in range(j + 1, 8):
                scaled = jnp.broadcast_to(edge[i][j : j + 1, :], (8, n)) * pivot
                edge[i] = jnp.where(mine, scaled, edge[i] - factor * scaled)
        solved = w
        w = [jnp.broadcast_to(solved[j : j + 1, :], (8, n)) for j in range(8)]
        fresh = []
        for r, t in enumerate(tiles):
            if r == kb:
                x = solved
            else:
                x = jnp.where(inside, 0.0, t)
                col = [jnp.broadcast_to(t[:, k + j : k + j + 1], (8, n)) for j in range(8)]
                pairs = [col[j] * w[j] + col[j + 1] * w[j + 1] for j in range(0, 8, 2)]
                x = x - ((pairs[0] + pairs[1]) + (pairs[2] + pairs[3]))
            fresh.append(x)
        tiles = fresh
    return jnp.concatenate(tiles, axis=0)


def dot(a, b, dims=((1,), (0,)), precision=HIGHEST):
    return lax.dot_general(
        a, b, (dims, ((), ())), precision=precision, preferred_element_type=jnp.float32
    )


def choices(picked, count):
    rank = picked.shape[1]
    index = lax.broadcasted_iota(jnp.int32, (count, rank), 0)
    chosen = index == picked
    ahead = jnp.sum((picked < index).astype(jnp.float32), axis=1, keepdims=True)
    member = jnp.sum(chosen.astype(jnp.float32), axis=1, keepdims=True)
    place = index.astype(jnp.float32) - ahead
    slot = lax.broadcasted_iota(jnp.int32, (count, rank), 1).astype(jnp.float32)
    others = (slot == place) & (jnp.broadcast_to(member, place.shape) < 0.5)
    return chosen.astype(jnp.float32), others.astype(jnp.float32)


def inverse_kernel(gram_ref, out_ref):
    out_ref[...] = spd_inverse(gram_ref[...])


def finish_kernel(
    node_at, total_ref, inverse_ref, picked_ref, table_ref, leaf_ref, node_ref
):
    rank = total_ref.shape[1]
    cross = total_ref[rank:, :]
    index = lax.broadcasted_iota(jnp.int32, cross.shape, 0)
    choice = (index == table_ref[pl.ds(node_at[0], 1), :]).astype(jnp.float32)
    gram = dot(choice, cross, ((0,), (0,)))
    chosen, others = choices(picked_ref[...], leaf_ref.shape[0])
    leaf_ref[...] = chosen + dot(others, dot(total_ref[:rank, :], inverse_ref[...]))
    node_ref[...] = dot(cross, spd_inverse(gram))


def unit_rows(matrix_ref, hit, n_grp):
    rows = matrix_ref.shape[0]
    pieces = []
    for c in range(n_grp):
        piece = matrix_ref[:, c * rows : (c + 1) * rows]
        pieces.append(jnp.where(hit == c, jnp.zeros_like(piece), piece))
    return pieces


def sides(block, probes_ref, side, half):
    both = dot(block, probes_ref[...], precision=None)
    low, high = both[:, :half], both[:, half:]
    return jnp.where(side == 0, high, low), jnp.where(side == 0, low, high)


def plain_kernel(n_leaf, n_grp, mask, matrix_ref, probes_ref, send_ref, keep_ref):
    spot = (lax.axis_index("leaf") >> 1) ^ mask
    hit = lax.axis_index("grp") * n_leaf + 2 * spot + pl.program_id(0) - lax.axis_index("leaf") * n_grp
    block = jnp.concatenate(unit_rows(matrix_ref, hit, n_grp), axis=1)
    send_ref[...], keep_ref[...] = sides(block, probes_ref, lax.axis_index("leaf") & 1, send_ref.shape[1])


def ordered_kernel(n_leaf, n_grp, high, matrix_ref, probes_ref, picked_ref, *outs):
    step = pl.program_id(0)
    spot = (lax.axis_index("leaf") >> 1) ^ (high - step // 2)
    hit = lax.axis_index("grp") * n_leaf + 2 * spot + step % 2 - lax.axis_index("leaf") * n_grp
    rank, half = picked_ref.shape[2], outs[0].shape[1]
    chosen, others = choices(picked_ref[0], matrix_ref.shape[0])
    order = jnp.concatenate([chosen, others], axis=1).astype(jnp.bfloat16)
    block = jnp.concatenate(
        [
            dot(order, piece, ((0,), (0,)), None).astype(jnp.bfloat16)
            for piece in unit_rows(matrix_ref, hit, n_grp)
        ],
        axis=1,
    )
    away, home = sides(block, probes_ref, lax.axis_index("leaf") & 1, half)
    for j in range(len(outs) // 4):

        @pl.when(step // 2 == j)
        def _():
            at = pl.ds(pl.multiple_of(step % 2 * rank, rank), rank)
            outs[4 * j][at, :] = away[:rank]
            outs[4 * j + 1][at, :] = home[:rank]
            outs[4 * j + 2][at, :] = away[rank:]
            outs[4 * j + 3][at, :] = home[rank:]


def split_kernel(keep_ref, received_ref, picked_ref, first_ref, second_ref):
    total = keep_ref[...] + received_ref[...]
    order = jnp.concatenate(choices(picked_ref[0], total.shape[0]), axis=1).astype(jnp.bfloat16)
    moved = None
    for _ in range(3):
        part = total.astype(jnp.bfloat16)
        total = total - part.astype(jnp.float32)
        value = dot(order, part, ((0,), (0,)), None)
        moved = value if moved is None else moved + value
    rank = first_ref.shape[0]
    first_ref[...] = moved[:rank]
    second_ref[...] = moved[rank:]


def on_device(matrix, probes, leaf_skeleton, node_skeleton):
    n_grp = lax.axis_size("grp")
    n_leaf = lax.axis_size("leaf")
    grp_pos = lax.axis_index("grp")
    leaf_pos = lax.axis_index("leaf")
    device = grp_pos * n_leaf + leaf_pos
    side = leaf_pos & 1
    spot = leaf_pos >> 1
    spots = n_leaf // 2
    row_count, col_count = matrix.shape
    leaf_rows = row_count // n_leaf
    half = probes.shape[1] // 2
    rank = leaf_skeleton.shape[1]
    all_leaves = n_grp * n_leaf
    leaf_bits, grp_bits = bits_of(n_leaf), bits_of(n_grp)
    levels = leaf_bits + grp_bits

    def across(value):
        return lax.ppermute(value, "leaf", [(p, p ^ 1) for p in range(n_leaf)])

    def along(value, hops):
        pairs = [(2 * a + s, 2 * b + s) for a, b in hops for s in range(2)]
        return lax.ppermute(value, "leaf", pairs)

    masks = list(range(spots - 1, -1, -1))
    top = masks[0]
    wide = jax.ShapeDtypeStruct((2 * leaf_rows, half), jnp.float32)
    slim = jax.ShapeDtypeStruct((2 * rank, half), jnp.float32)

    def leaf_row(high):
        return lambda i: 2 * ((lax.axis_index("leaf") >> 1) ^ (high - i // 2)) + i % 2

    def grid_spec(count, in_specs, out_specs):
        return pl.GridSpec(grid=(count,), in_specs=in_specs, out_specs=out_specs)

    def matrix_specs(high):
        row = leaf_row(high)
        return [
            pl.BlockSpec((leaf_rows, col_count), lambda i: (row(i), 0)),
            pl.BlockSpec(memory_space=pltpu.VMEM),
        ]

    def picked_spec(high):
        row = leaf_row(high)
        return pl.BlockSpec((1, 1, rank), lambda i: (row(i), 0, 0))

    send, keep = pl.pallas_call(
        lambda *refs: plain_kernel(n_leaf, n_grp, top, *refs),
        out_shape=(wide,) * 2,
        grid_spec=grid_spec(
            2, matrix_specs(top), [pl.BlockSpec((leaf_rows, half), lambda i: (i, 0))] * 2
        ),
        name="product",
    )(matrix, probes)

    skeletons = leaf_skeleton
    for bit in range(leaf_bits):
        partner = lax.ppermute(skeletons, "leaf", [(p, p ^ 1 << bit) for p in range(n_leaf)])
        if bit == 0:
            send, partner = lax.optimization_barrier((send, partner))
        skeletons = jnp.where(
            leaf_pos >> bit & 1 == 1,
            jnp.concatenate([partner, skeletons], axis=0),
            jnp.concatenate([skeletons, partner], axis=0),
        )
    top_received = across(send)
    tables = skeletons[:, None, :]

    def ordered(group):
        high, count = group[0], len(group)
        outs = pl.pallas_call(
            lambda *refs: ordered_kernel(n_leaf, n_grp, high, *refs),
            out_shape=(slim,) * (4 * count),
            grid_spec=grid_spec(
                2 * count,
                [*matrix_specs(high), picked_spec(high)],
                [pl.BlockSpec(slim.shape, lambda i: (0, 0))] * (4 * count),
            ),
            name="ordered",
        )
        outs = outs(matrix, probes, tables)
        return {mask: outs[4 * j : 4 * j + 4] for j, mask in enumerate(group)}

    pieces = {}
    for at in range(1, spots, GROUP):
        pieces.update(ordered(masks[at : at + GROUP]))

    piece = pl.BlockSpec((leaf_rows, half), lambda i: (i, 0))
    part = pl.BlockSpec((rank, half), lambda i: (i, 0))
    first, second = {}, {}
    split = pl.pallas_call(
        split_kernel,
        out_shape=(slim,) * 2,
        grid_spec=grid_spec(2, [piece, piece, picked_spec(top)], [part] * 2),
        name="split",
    )
    first[top], second[top] = split(keep, top_received, tables)

    for mask in masks[1:]:
        received = across(pieces[mask][0])
        first[mask] = pieces[mask][1] + received
        if mask == min(1, top):
            gate = received
    for mask in masks[1:]:
        send, _ = lax.optimization_barrier((pieces[mask][2], gate))
        second[mask] = pieces[mask][3] + across(send)

    def gathered(values, gates=None):
        values = dict(values)
        for mask in masks[:-1]:
            bit = mask & -mask
            value = values[mask]
            if gates is not None:
                gate = gates[0] if mask == top else gates[1]
                value, _ = lax.optimization_barrier((value, gate))
            elif mask ^ bit == 0:
                early.append(value)
            arrived = along(
                value, [(z, z ^ bit) for z in range(spots)]
            )
            if gates is not None and mask != top:
                arrived, _ = lax.optimization_barrier((arrived, gates[2]))
            values[mask ^ bit] = values[mask ^ bit] + arrived
        return values[0]

    early = []

    skeleton_rows = gathered(first)

    def cross_of(stacked, rows):
        return dot(stacked, rows, ((1,), (1,)))

    halves = (skeleton_rows[:rank], skeleton_rows[rank:])
    grams = [cross_of(r, r) for r in halves]
    own_gram = jnp.where(side == 0, grams[0], grams[1])
    received_gram = across(jnp.where(side == 0, grams[1], grams[0]))

    def level_offset(level):
        return sum(all_leaves >> inner for inner in range(1, level))

    def picked_of(level):
        node = level_offset(level) + (device >> level)
        return lax.dynamic_slice_in_dim(node_skeleton, node, 1, 0)[0]

    gates = []

    def taken(stacked, picked):
        index = jnp.arange(stacked.shape[0], dtype=jnp.int32)
        return dot((picked[:, None] == index[None, :]).astype(jnp.float32), stacked)

    low_stack = skeleton_rows
    low_picked = picked_of(1)
    node_own = device >> 1
    current = taken(low_stack, low_picked)
    low_cross = high_cross = cross_of(low_stack, current)
    even = device - side
    for level in range(2, levels + 1):
        if level <= leaf_bits:
            bit = level - 2
            hops = [(z, z ^ 1 << bit) for z in range(0, spots, 1 << bit)]
            partner = along(current, hops)
            upper = spot >> bit & 1
            gates.append(partner)
        else:
            bit = level - leaf_bits - 1
            pairs = [
                (g * n_leaf + s, (g ^ 1 << bit) * n_leaf + s)
                for g in range(0, n_grp, 1 << bit)
                for s in range(2)
            ]
            send = lambda value: lax.ppermute(value, ("grp", "leaf"), pairs)
            partner = send(current)
            upper = grp_pos >> bit & 1
        before = current
        if level == levels:
            partner, gram = lax.optimization_barrier((partner, own_gram + received_gram))
        stacked = jnp.concatenate(
            [
                jnp.where(upper == 1, partner, current),
                jnp.where(upper == 1, current, partner),
            ],
            axis=0,
        )
        picked = picked_of(level)
        current = taken(stacked, picked)
        select = even % (1 << level) == 1 << level - 1
        if level == levels:
            select = select | (even == 0)
        high_cross = jnp.where(select, cross_of(stacked, current), high_cross)
        node = level_offset(level) + (device >> level)
        node_own = jnp.where(select & (side == 0), node, node_own)

    other_rows = gathered(second, [early[0], gates[0], before])
    crosses = [
        cross_of(z, r) for z, r in zip((other_rows[:rank], other_rows[rank:]), halves)
    ]
    sent = jnp.concatenate(
        [
            jnp.where(side == 0, crosses[1], crosses[0]),
            jnp.where(side == 1, high_cross, low_cross),
        ],
        axis=0,
    )
    received = across(sent)
    own = jnp.concatenate(
        [
            jnp.where(side == 0, crosses[0], crosses[1]),
            jnp.where(side == 1, low_cross, high_cross),
        ],
        axis=0,
    )
    total = own + received
    square = jax.ShapeDtypeStruct((rank, rank), jnp.float32)
    inverse = pl.pallas_call(inverse_kernel, out_shape=square, name="inverse")(gram)
    tall = [jax.ShapeDtypeStruct((rows, rank), jnp.float32) for rows in (leaf_rows, 2 * rank)]
    whole = pl.BlockSpec(memory_space=pltpu.VMEM)
    leaf_basis, transfer = pl.pallas_call(
        finish_kernel,
        out_shape=tall,
        in_specs=[pl.BlockSpec(memory_space=pltpu.SMEM)] + [whole] * 4,
        name="finish",
    )(
        node_own[None], total, inverse, leaf_skeleton, node_skeleton
    )
    return (leaf_basis, transfer[None])


def solution(mesh):
    return jax.shard_map(
        on_device,
        mesh=mesh,
        in_specs=(P("grp", "leaf"), P("leaf", None), P(("grp", "leaf"), None), P()),
        out_specs=(P(("grp", "leaf"), None), P(("grp", "leaf"), None, None)),
        check_vma=False,
    )
```
